256 devices in a mesh: ens: 16 (over x_hi, z), lon: 4 (over x_lo, core), lat: 4 (over y).
Axes of the slice: x: 4 (x_hi: 2, x_lo: 2; x = x_hi * 2 + x_lo), y: 4, z: 8, core: 2. Of those that a mesh axis runs over, the one named last changes fastest.
Arguments:
- members: float32 [16, 80, 32, 640], P('ens', 'lat', 'lon'), may hold values from -6 to 6
- analysis: float32 [80, 32, 640], P('lat', 'lon', 'ens'), may hold values from -6 to 6
- stencils: float32 [7, 7, 7, 80], replicated, may hold values from -0.84 to 0.84
- mixing: float32 [7, 640, 640], replicated, may hold values from -0.09375 to 0.09375
Outputs:
- members_grad: float32 [16, 80, 32, 640], P('ens', 'lat', 'lon')
- crps_field: float32 [80, 32, 640], P('lat', 'lon', 'ens')
The draws below stay inside these ranges and needn't reach their ends.
All inputs are finite; a program needn't handle non-finite values.
Results may differ from the reference program's by a relative error of at most 0.00016.
Values sent between devices are 32-bit elements; how exact they have to be, the bound alone decides.
A program may use at most 128 MiB of HBM per device.

```python
import jax
import jax.numpy as jnp
from jax import lax

C = 640
BASES = 7
SPAN = 7
MEMBERS = 16
LAT_ROWS = 80
LON_COLS = 32


def level_of(stream_key, shape, pieces, least, top_value):
    def one(dim, shards_of):
        heights = jax.random.uniform(jax.random.fold_in(jax.random.fold_in(stream_key, 6), dim), (shards_of,), jnp.float32, least / len(pieces), top_value / len(pieces))
        return jnp.repeat(jnp.exp(heights), shape[dim] // shards_of).reshape((-1,) + (1,) * (len(shape) - dim - 1))

    level = one(*pieces[0])
    for cut in pieces[1:]:
        level = level * one(*cut)
    return level


def centred(key, dims, width, most, cuts=(), held_as=jnp.bfloat16):
    gain = level_of(key, dims, cuts, -0.22, 0.18) if cuts else 1.0
    entries = jax.random.normal(key, dims, jnp.float32) * width * gain
    return jnp.minimum(jnp.maximum(entries, -most), most).astype(held_as)


def setup_inputs(seed: int = 0) -> dict:
    streams_of = jax.random.split(jax.random.key(seed), 5)
    members = centred(streams_of[0], (MEMBERS, LAT_ROWS, LON_COLS, C), 1.0, 6.0, ((0, 16), (1, 4), (2, 4)), jnp.float32)
    analysis = centred(streams_of[1], (LAT_ROWS, LON_COLS, C), 1.0, 6.0, ((0, 4), (1, 4), (2, 16)), jnp.float32)
    stencils = centred(streams_of[2], (BASES, SPAN, SPAN, LAT_ROWS), 0.14, 0.84, (), jnp.float32)
    mixing = centred(streams_of[3], (BASES, C, C), (BASES * C) ** -0.5, 0.09375, (), jnp.float32)
    return dict(members=members, analysis=analysis, stencils=stencils, mixing=mixing)


smooth = 0.01
highest = lax.Precision.HIGHEST

def soft_abs(values):
    return jnp.sqrt(values * values + smooth)

def extend_field(field_block):
    margin = SPAN // 2
    wrapped = jnp.concatenate([field_block[:, -margin:], field_block, field_block[:, :margin]], axis=1)
    return jnp.pad(wrapped, ((margin, margin), (0, 0), (0, 0)))

def tap_sum(extended, weights):
    height = weights.shape[3]
    breadth = extended.shape[1] - SPAN + 1
    running = jnp.zeros((weights.shape[0], height, breadth, extended.shape[2]), jnp.float32)
    for row_tap in range(SPAN):
        for col_tap in range(SPAN):
            running = running + weights[:, row_tap, col_tap, :, None, None] * extended[None, row_tap:row_tap + height, col_tap:col_tap + breadth, :]
    return running

def reference(members, analysis, stencils, mixing):
    margin = SPAN // 2
    height = stencils.shape[3]
    padded = jnp.pad(stencils, ((0, 0), (0, 0), (0, 0), (margin, margin)))
    forward = padded[:, :, :, margin:margin + height]
    backward = jnp.stack([padded[:, SPAN - 1 - row_tap, ::-1, row_tap:row_tap + height] for row_tap in range(SPAN)], axis=1)

    def predict_single_member(member_index):
        mixed = jnp.einsum('bhwc,bco->hwo', tap_sum(extend_field(member_index), forward), mixing, precision=highest)
        bounded_activation = jnp.tanh(mixed)
        return (member_index + bounded_activation, bounded_activation)
    predicted_fields, bounded_activation = lax.map(predict_single_member, members)
    prediction_error = predicted_fields - analysis[None]

    def pair_step(other_member, totals):
        differ = prediction_error - lax.dynamic_index_in_dim(prediction_error, other_member, 0, keepdims=False)
        smooth_abs = soft_abs(differ)
        return (totals[0] + smooth_abs, totals[1] + differ / smooth_abs)
    zero_sums = jnp.zeros_like(prediction_error)
    sum_abs, sum_slope = lax.fori_loop(0, MEMBERS, pair_step, (zero_sums, zero_sums))
    own_abs = soft_abs(prediction_error)
    crps_field = lax.optimization_barrier(jnp.mean(own_abs, 0)) - lax.optimization_barrier(jnp.sum(sum_abs, 0)) / (2.0 * MEMBERS * (MEMBERS - 1))
    grad_out = prediction_error / own_abs - sum_slope / (MEMBERS - 1.0)
    inner_grad = grad_out * (1.0 - bounded_activation * bounded_activation)

    def adjoint_one(pair_args):
        outer_grad, inner_one = pair_args
        spread = tap_sum(extend_field(inner_one), backward)
        return outer_grad + jnp.einsum('bhwo,bco->hwc', spread, mixing, precision=highest)
    members_grad = lax.map(adjoint_one, (grad_out, inner_grad))
    return (members_grad, crps_field)
```

```python
import functools

import jax
import jax.numpy as jnp
import numpy as np
from jax import lax
from jax.experimental import pallas as pl
from jax.experimental.pallas import tpu as pltpu
from jax.sharding import PartitionSpec as P

BASES = 7
SPAN = 7
MARGIN = 3
ROWS = 20
COLS = 8
WINDOWS = ROWS // 2
EXT = ROWS + 2 * MARGIN
SMOOTH = 0.01
MESH = pl.DeviceIdType.MESH
f32 = jnp.float32
bf16 = jnp.bfloat16


def split(x):
    hi = x.astype(bf16)
    return hi, (x - hi.astype(f32)).astype(bf16)


def mm(a, b):
    return jnp.dot(a, b, preferred_element_type=f32)


def prep_kernel(st_ref, fh_ref, fl_ref, bh_ref, bl_ref, spaced, by_row):
    lat_rows = st_ref.shape[3]
    first = lax.axis_index("lat") * ROWS
    lane = lax.broadcasted_iota(jnp.int32, (8, 128), 1)
    wrapped = (lane % 16) >= 11
    spaced[...] = jnp.zeros_like(spaced)

    def one_basis(b, carry):
        for p in range(SPAN):
            spaced[0, 16 * p : 16 * p + SPAN, 0:lat_rows] = st_ref[b, p]
            for q in range(SPAN):
                r = 16 * p + q
                spaced[1, r : r + 1, 0:lat_rows] = st_ref[b, SPAN - 1 - p, SPAN - 1 - q : SPAN - q, :]
        by_row[0] = pltpu.roll(spaced[0].T, 128 - MARGIN, 1)
        moved = [pltpu.roll(spaced[1, 16 * p : 16 * p + 16, :], (MARGIN - p) % 128, 1) for p in range(8)]
        by_row[1] = pltpu.roll(jnp.concatenate(moved, axis=0).T, 128 - MARGIN, 1)

        def one_window(u, carry):
            for kind, hi_ref, lo_ref in ((0, fh_ref, fl_ref), (1, bh_ref, bl_ref)):
                rows = []
                for i01 in range(2):
                    line = by_row[kind, pl.ds(first + 2 * u + i01, 1), :]
                    line = jnp.broadcast_to(line, (8, 128))
                    shifted = pltpu.roll(line, 16 * i01, 1, stride=1, stride_axis=0)
                    rows.append(jnp.where(wrapped, pltpu.roll(shifted, 16, 1), shifted))
                hi, lo = split(jnp.concatenate(rows, axis=0))
                at = pl.ds(pl.multiple_of(16 * b, 16), 16)
                hi_ref[u, at, :] = hi
                lo_ref[u, at, :] = lo
            return carry

        return lax.fori_loop(0, WINDOWS, one_window, carry)

    lax.fori_loop(0, BASES, one_basis, 0)


def stencil_matrices(stencils):
    shape = jax.ShapeDtypeStruct((WINDOWS, 16 * BASES, 128), bf16)
    return pl.pallas_call(
        prep_kernel,
        out_shape=[shape] * 4,
        in_specs=[pl.BlockSpec(memory_space=pltpu.VMEM)],
        out_specs=[pl.BlockSpec(memory_space=pltpu.VMEM)] * 4,
        scratch_shapes=[pltpu.VMEM((2, 128, 128), f32), pltpu.VMEM((2, 128, 128), f32)],
        name="stencil_matrices",
    )(stencils)


def pack_tile(dst, tile, t, part, rows):
    if part == 0:
        dst[rows, 8 * t : 8 * t + 8, :] = tile
    else:
        base = dst.shape[1] - 16 + 8 * (t // 4)
        g = t % 4
        dst[rows, base : base + 8, 32 * g : 32 * g + 32] = tile


def tail_of(src, t, piece):
    base = src.shape[1] - 16 + 8 * (t // 4)
    g = t % 4
    return src[piece, base : base + 8, 32 * g : 32 * g + 32]


def step_kernel(
    members_ref, analysis_ref, fh_ref, fl_ref, bh_ref, bl_ref, mixing_ref,
    grad_ref, crps_ref,
    staged, m_hi, m_lo, e_hi, e_lo, s_hi, s_lo, field, damp, pack_r, pack_l,
    side, updown, corner, a_pack, c_pack, send1, recv1, send2, recv2,
    mix_sem, halo_send, halo_recv, a2a_send, a2a_recv,
):
    n_ens = lax.axis_size("ens")
    n_lat = lax.axis_size("lat")
    n_lon = lax.axis_size("lon")
    ens, lat, lon = lax.axis_index("ens"), lax.axis_index("lat"), lax.axis_index("lon")
    right, left = lax.rem(lon + 1, n_lon), lax.rem(lon + n_lon - 1, n_lon)
    has_up, has_down = lat > 0, lat < n_lat - 1
    channels = members_ref.shape[2]
    depth = BASES * channels
    tiles = channels // n_ens // 8

    for b in range(BASES):
        pltpu.make_async_copy(mixing_ref.at[b], staged.at[b], mix_sem.at[b]).start()

    barrier = pltpu.get_barrier_semaphore()

    def greet(k, carry):
        pl.semaphore_signal(barrier, 1, device_id={"ens": lax.rem(ens + k, n_ens)}, device_id_type=MESH)
        return carry

    lax.fori_loop(1, n_ens, greet, 0)
    for side_lon in (left, right):
        pl.semaphore_signal(barrier, 1, device_id={"lon": side_lon}, device_id_type=MESH)
    for there, other in ((has_up, lat - 1), (has_down, lat + 1)):
        @pl.when(there)
        def _():
            pl.semaphore_signal(barrier, 1, device_id={"lat": other}, device_id_type=MESH)
            for side_lon in (left, right):
                pl.semaphore_signal(barrier, 1, device_id={"lat": other, "lon": side_lon}, device_id_type=MESH)

    def fill_packs(src):
        for r in range(ROWS):
            pack_r[3 * r : 3 * r + 3, :] = src[r, COLS - MARGIN : COLS, :]
            pack_l[3 * r : 3 * r + 3, :] = src[r, 0:MARGIN, :]

    pack_r[56:64, :] = jnp.zeros((8, channels), f32)
    pack_l[56:64, :] = jnp.zeros((8, channels), f32)
    fill_packs(members_ref)
    pl.semaphore_wait(barrier, n_ens + 1 + 3 * has_up.astype(jnp.int32) + 3 * has_down.astype(jnp.int32))

    def halo_copies(phase, src):
        def remote(k, a, b, to):
            return pltpu.make_async_remote_copy(
                a, b, halo_send.at[phase, k], halo_recv.at[phase, k], device_id=to, device_id_type=MESH
            )

        up, down = lat - 1, lat + 1
        low = pl.ds(0, 16)
        high = pl.ds(48, 16)
        return [
            (None, None, remote(0, pack_r, side.at[phase, 0], {"lon": right})),
            (None, None, remote(1, pack_l, side.at[phase, 1], {"lon": left})),
            (has_down, has_up, remote(2, src.at[pl.ds(ROWS - 3, 3)], updown.at[phase, 0], {"lat": down})),
            (has_up, has_down, remote(3, src.at[pl.ds(0, 3)], updown.at[phase, 1], {"lat": up})),
            (has_down, has_up, remote(4, pack_r.at[high], corner.at[phase, 0], {"lat": down, "lon": right})),
            (has_down, has_up, remote(5, pack_l.at[high], corner.at[phase, 1], {"lat": down, "lon": left})),
            (has_up, has_down, remote(6, pack_r.at[low], corner.at[phase, 2], {"lat": up, "lon": right})),
            (has_up, has_down, remote(7, pack_l.at[low], corner.at[phase, 3], {"lat": up, "lon": left})),
        ]

    def start_halo(phase, src):
        for sends, _, copy in halo_copies(phase, src):
            if sends is None:
                copy.start()
            else:
                pl.when(sends)(copy.start)

    def put_row(r, inner, from_right, from_left):
        hi, lo = split(
            jnp.concatenate([inner, from_right, jnp.zeros((2, channels), f32), from_left], axis=0)
        )
        e_hi[16 * r : 16 * r + 16, :] = hi
        e_lo[16 * r : 16 * r + 16, :] = lo

    def extend(phase, src):
        copies = halo_copies(phase, src)
        for k in (0, 1):
            copies[k][2].wait()
        for r in range(ROWS):
            at = slice(3 * r, 3 * r + 3)
            put_row(r + MARGIN, src[r], side[phase, 1, at, :], side[phase, 0, at, :])
        for there, which, corners, first, offset in (
            (has_up, 0, (0, 1), 0, 3),
            (has_down, 1, (2, 3), ROWS + MARGIN, 0),
        ):
            @pl.when(there)
            def _():
                for k in (2 + which, 4 + 2 * which, 5 + 2 * which):
                    copies[k][2].wait_recv()
                for r in range(3):
                    at = slice(offset + 3 * r, offset + 3 * r + 3)
                    put_row(
                        first + r, updown[phase, which, r],
                        corner[phase, corners[1], at, :], corner[phase, corners[0], at, :],
                    )

            @pl.when(jnp.logical_not(there))
            def _():
                for ref in (e_hi, e_lo):
                    ref[16 * first : 16 * first + 48, :] = jnp.zeros((48, channels), bf16)
        for k in range(2, 8):
            pl.when(copies[k][0])(copies[k][2].wait_send)

    def stencil(w_hi, w_lo):
        def one_window(u, carry):
            at = pl.ds(pl.multiple_of(32 * u, 32), 128)
            x_hi, x_lo = e_hi[at, :], e_lo[at, :]
            wh = w_hi[u]
            out = mm(jnp.concatenate([wh, wh], axis=1), jnp.concatenate([x_hi, x_lo], axis=0)) + mm(w_lo[u], x_hi)
            hi, lo = split(out)
            to = pl.ds(pl.multiple_of(16 * u, 16), 16)
            for b in range(BASES):
                s_hi[to, b * channels : (b + 1) * channels] = hi[16 * b : 16 * b + 16]
                s_lo[to, b * channels : (b + 1) * channels] = lo[16 * b : 16 * b + 16]
            return carry

        lax.fori_loop(0, WINDOWS, one_window, 0)

    def mix(cols):
        weights = m_hi[:, cols]
        return mm(s_hi[...], weights) + mm(s_lo[...], weights) + mm(s_hi[...], m_lo[:, cols])

    def chunks():
        return [slice(c, min(c + 256, channels)) for c in range(0, channels, 256)]

    def load_weights(b, carry):
        pltpu.make_async_copy(mixing_ref.at[b], staged.at[b], mix_sem.at[b]).wait()

        def part(k, carry):
            rows = pl.ds(pl.multiple_of(128 * k, 128), 128)
            hi, lo = split(staged[b, rows, :])
            to = pl.ds(pl.multiple_of(b * channels + 128 * k, 128), 128)
            m_hi[to, :] = hi
            m_lo[to, :] = lo
            return carry

        return lax.fori_loop(0, channels // 128, part, carry)

    def transpose_weights(b, carry):
        def part(k, carry):
            cols = pl.ds(pl.multiple_of(128 * k, 128), 128)
            hi, lo = split(staged[b, :, cols].T)
            to = pl.ds(pl.multiple_of(b * channels + 128 * k, 128), 128)
            m_hi[to, :] = hi
            m_lo[to, :] = lo
            return carry

        return lax.fori_loop(0, channels // 128, part, carry)

    start_halo(0, members_ref)

    zero_piece = jnp.zeros((16, 128), f32)
    a_pack[0, 8 * tiles : 8 * tiles + 16, :] = zero_piece
    truth = jnp.concatenate(
        [analysis_ref[...].reshape(ROWS * COLS, 8 * tiles), jnp.zeros((ROWS * COLS, 128 - 8 * tiles), f32)], axis=1
    )
    main, tail = truth[:128].T, jnp.concatenate([truth[128:], jnp.zeros((96, 128), f32)], axis=0).T
    for t in range(tiles):
        pack_tile(a_pack, main[8 * t : 8 * t + 8], t, 0, 0)
        pack_tile(a_pack, tail[8 * t : 8 * t + 8, 0:32], t, 1, 0)

    lax.fori_loop(0, BASES, load_weights, 0)
    extend(0, members_ref)
    stencil(fh_ref, fl_ref)

    for d in range(n_ens):
        send1[d, 8 * tiles : 8 * tiles + 16, :] = zero_piece
    for cols in chunks():
        width = cols.stop - cols.start
        activation = jnp.tanh(mix(cols))
        damp[:, cols] = 1.0 - activation * activation
        forecast = members_ref[:, :, cols].reshape(ROWS * COLS, width) + activation
        for c in range(width // 128):
            part = forecast[:, 128 * c : 128 * c + 128]
            main = part[:128].T
            tail = jnp.concatenate([part[128:], jnp.zeros((96, 128), f32)], axis=0).T
            for s in range(16):
                k = (cols.start // 128 + c) * 16 + s
                pack_tile(send1, main[8 * s : 8 * s + 8], k % tiles, 0, k // tiles)
                pack_tile(send1, tail[8 * s : 8 * s + 8, 0:32], k % tiles, 1, k // tiles)

    def exchange(phase, src, dst, other, slot):
        return pltpu.make_async_remote_copy(
            src.at[other], dst.at[slot], a2a_send.at[phase, other], a2a_recv.at[phase, slot],
            device_id={"ens": other}, device_id_type=MESH,
        )

    def start_all(phase, src, dst):
        def start(k, carry):
            exchange(phase, src, dst, lax.rem(ens + k, n_ens), ens).start()
            return carry

        lax.fori_loop(1, n_ens, start, 0)
        dst[ens] = src[ens]

    def wait_all(phase, src, dst):
        def wait(k, carry):
            other = lax.rem(ens + k, n_ens)
            exchange(phase, src, dst, other, other).wait_recv()
            exchange(phase, src, dst, other, ens).wait_send()
            return carry

        lax.fori_loop(1, n_ens, wait, 0)

    start_all(0, send1, recv1)
    lax.fori_loop(0, BASES, transpose_weights, 0)
    wait_all(0, send1, recv1)

    members_total = n_ens
    diagonal = members_total * float(np.sqrt(np.float32(SMOOTH)))
    pairs_scale = 2.0 * members_total * (members_total - 1)

    def score(t, carry):
        rows = pl.ds(pl.multiple_of(8 * t, 8), 8)
        truth = a_pack[0, rows, :]
        x = [recv1[m, rows, :] - truth for m in range(n_ens)]
        slope = [None] * n_ens
        own, pair_abs = None, None
        for m in range(n_ens):
            for n in range(m + 1, n_ens):
                d = x[m] - x[n]
                s2 = d * d + SMOOTH
                r = lax.rsqrt(s2)
                sl = d * r
                ab = s2 * r
                pair_abs = ab if pair_abs is None else pair_abs + ab
                slope[m] = sl if slope[m] is None else slope[m] + sl
                slope[n] = -sl if slope[n] is None else slope[n] - sl
            s2 = x[m] * x[m] + SMOOTH
            r = lax.rsqrt(s2)
            own = s2 * r if own is None else own + s2 * r
            send2[m, rows, :] = x[m] * r - slope[m] * (1.0 / (members_total - 1.0))
        c_pack[0, rows, :] = own * (1.0 / members_total) - (2.0 * pair_abs + diagonal) * (1.0 / pairs_scale)
        return carry

    lax.fori_loop(0, tiles + 2, score, 0)
    start_all(1, send2, recv2)

    main = jnp.concatenate(
        [c_pack[0, 8 * t : 8 * t + 8, :] for t in range(tiles)] + [jnp.zeros((128 - 8 * tiles, 128), f32)], axis=0
    ).T
    crps_ref[0:16] = main[:, 0 : 8 * tiles].reshape(16, COLS, 8 * tiles)
    tail = jnp.concatenate([tail_of(c_pack, t, 0) for t in range(tiles)], axis=0)
    tail = jnp.concatenate([tail, jnp.zeros((8 * tiles, 96), f32)], axis=1)
    tail = jnp.concatenate([tail, jnp.zeros((128 - 8 * tiles, 128), f32)], axis=0).T
    crps_ref[16:20] = tail[0:32, 0 : 8 * tiles].reshape(4, COLS, 8 * tiles)

    wait_all(1, send2, recv2)

    for c in range(channels // 128):
        mains, tails = [], []
        for s in range(16):
            k = c * 16 + s
            piece, t = k // tiles, k % tiles
            mains.append(recv2[piece, 8 * t : 8 * t + 8, :])
            tails.append(tail_of(recv2, t, piece))
        main = jnp.concatenate(mains, axis=0).T
        tail = jnp.concatenate([jnp.concatenate(tails, axis=0), jnp.zeros((128, 96), f32)], axis=1).T
        cols = slice(128 * c, 128 * c + 128)
        grad_ref[0:16, :, cols] = main.reshape(16, COLS, 128)
        grad_ref[16:20, :, cols] = tail[0:32].reshape(4, COLS, 128)
    field[...] = grad_ref[...] * damp[...].reshape(ROWS, COLS, channels)
    fill_packs(field)
    start_halo(1, field)
    extend(1, field)
    stencil(bh_ref, bl_ref)
    for cols in chunks():
        width = cols.stop - cols.start
        grad_ref[:, :, cols] = grad_ref[:, :, cols] + mix(cols).reshape(ROWS, COLS, width)


def local(members, analysis, stencils, mixing):
    channels = members.shape[3]
    n_ens = lax.axis_size("ens")
    per = channels // n_ens
    depth = BASES * channels
    cells = ROWS * COLS
    piece = (n_ens, per + 16, 128)
    matrices = stencil_matrices(stencils)
    vmem = pl.BlockSpec(memory_space=pltpu.VMEM)
    grad, crps = pl.pallas_call(
        step_kernel,
        out_shape=[
            jax.ShapeDtypeStruct((ROWS, COLS, channels), f32),
            jax.ShapeDtypeStruct((ROWS, COLS, per), f32),
        ],
        in_specs=[vmem] * 6 + [pl.BlockSpec(memory_space=pl.ANY)],
        out_specs=[vmem, vmem],
        scratch_shapes=[
            pltpu.VMEM((BASES, channels, channels), f32),
            pltpu.VMEM((depth, channels), bf16),
            pltpu.VMEM((depth, channels), bf16),
            pltpu.VMEM((16 * EXT, channels), bf16),
            pltpu.VMEM((16 * EXT, channels), bf16),
            pltpu.VMEM((cells, depth), bf16),
            pltpu.VMEM((cells, depth), bf16),
            pltpu.VMEM((ROWS, COLS, channels), f32),
            pltpu.VMEM((cells, channels), f32),
            pltpu.VMEM((64, channels), f32),
            pltpu.VMEM((64, channels), f32),
            pltpu.VMEM((2, 2, 64, channels), f32),
            pltpu.VMEM((2, 2, MARGIN, COLS, channels), f32),
            pltpu.VMEM((2, 4, 16, channels), f32),
            pltpu.VMEM((1, per + 16, 128), f32),
            pltpu.VMEM((1, per + 16, 128), f32),
            pltpu.VMEM(piece, f32),
            pltpu.VMEM(piece, f32),
            pltpu.VMEM(piece, f32),
            pltpu.VMEM(piece, f32),
            pltpu.SemaphoreType.DMA((BASES,)),
            pltpu.SemaphoreType.DMA((2, 8)),
            pltpu.SemaphoreType.DMA((2, 8)),
            pltpu.SemaphoreType.DMA((2, n_ens)),
            pltpu.SemaphoreType.DMA((2, n_ens)),
        ],
        compiler_params=pltpu.CompilerParams(
            collective_id=0, has_side_effects=True, vmem_limit_bytes=56 * 1024 * 1024
        ),
        name="ensemble_step",
    )(members[0], analysis, *matrices, mixing)
    return grad[None], crps


def solution(mesh):
    in_specs = (P("ens", "lat", "lon", None), P("lat", "lon", "ens"), P(), P())
    out_specs = (P("ens", "lat", "lon", None), P("lat", "lon", "ens"))
    return jax.shard_map(local, mesh=mesh, in_specs=in_specs, out_specs=out_specs, check_vma=False)
```

```python
import functools

import jax
import jax.numpy as jnp
import numpy as np
from jax import lax
from jax.experimental import pallas as pl
from jax.experimental.pallas import tpu as pltpu
from jax.sharding import PartitionSpec as P

BASES = 7
SPAN = 7
MARGIN = 3
ROWS = 20
COLS = 8
WINDOWS = ROWS // 2
EXT = ROWS + 2 * MARGIN
SMOOTH = 0.01
MESH = pl.DeviceIdType.MESH
f32 = jnp.float32
bf16 = jnp.bfloat16


def split(x):
    hi = x.astype(bf16)
    return hi, (x - hi.astype(f32)).astype(bf16)


def mm(a, b):
    return jnp.dot(a, b, preferred_element_type=f32)


def stencil_matrices(kind, st_ref, hi_ref, lo_ref, spaced, by_row):
    lat_rows = st_ref.shape[3]
    first = lax.axis_index("lat") * ROWS
    lane = lax.broadcasted_iota(jnp.int32, (8, 128), 1)
    wrapped = (lane % 16) >= 11
    spaced[...] = jnp.zeros_like(spaced)

    def one_basis(b, carry):
        for p in range(SPAN):
            if kind == 0:
                spaced[16 * p : 16 * p + SPAN, 0:lat_rows] = st_ref[b, p]
            else:
                for q in range(SPAN):
                    r = 16 * p + q
                    spaced[r : r + 1, 0:lat_rows] = st_ref[b, SPAN - 1 - p, SPAN - 1 - q : SPAN - q, :]
        if kind == 0:
            lines = spaced[...]
        else:
            lines = jnp.concatenate(
                [pltpu.roll(spaced[16 * p : 16 * p + 16, :], (MARGIN - p) % 128, 1) for p in range(8)], axis=0
            )
        by_row[...] = pltpu.roll(lines.T, 128 - MARGIN, 1)
        at = pl.ds(pl.multiple_of(16 * b, 16), 16)
        for u in range(WINDOWS):
            rows = []
            for i01 in range(2):
                line = jnp.broadcast_to(by_row[pl.ds(first + 2 * u + i01, 1), :], (8, 128))
                shifted = pltpu.roll(line, 16 * i01, 1, stride=1, stride_axis=0)
                rows.append(jnp.where(wrapped, pltpu.roll(shifted, 16, 1), shifted))
            hi_ref[u, at, :], lo_ref[u, at, :] = split(jnp.concatenate(rows, axis=0))
        return carry

    lax.fori_loop(0, BASES, one_basis, 0)


def pack_tile(dst, tile, t, part, rows):
    if part == 0:
        dst[rows, 8 * t : 8 * t + 8, :] = tile
    else:
        base = dst.shape[1] - 16 + 8 * (t // 4)
        g = t % 4
        dst[rows, base : base + 8, 32 * g : 32 * g + 32] = tile


def tail_of(src, t, piece):
    base = src.shape[1] - 16 + 8 * (t // 4)
    g = t % 4
    return src[piece, base : base + 8, 32 * g : 32 * g + 32]


def step_kernel(
    members_ref, analysis_ref, stencils_ref, mixing_ref,
    grad_ref, crps_ref,
    w_hi, w_lo, spaced, by_row, staged, m_hi, m_lo, e_hi, e_lo, s_hi, s_lo, field, damp, pack_r, pack_l,
    side, updown, corner, a_pack, c_pack, send1, recv1, send2, recv2,
    mix_sem, halo_send, halo_recv, a2a_send, a2a_recv,
):
    n_ens = lax.axis_size("ens")
    n_lat = lax.axis_size("lat")
    n_lon = lax.axis_size("lon")
    ens, lat, lon = lax.axis_index("ens"), lax.axis_index("lat"), lax.axis_index("lon")
    right, left = lax.rem(lon + 1, n_lon), lax.rem(lon + n_lon - 1, n_lon)
    has_up, has_down = lat > 0, lat < n_lat - 1
    channels = members_ref.shape[2]
    depth = BASES * channels
    tiles = channels // n_ens // 8

    for b in range(BASES):
        pltpu.make_async_copy(mixing_ref.at[b], staged.at[b], mix_sem.at[b]).start()

    barrier = pltpu.get_barrier_semaphore()

    def greet(k, carry):
        pl.semaphore_signal(barrier, 1, device_id={"ens": lax.rem(ens + k, n_ens)}, device_id_type=MESH)
        return carry

    lax.fori_loop(1, n_ens, greet, 0)
    for side_lon in (left, right):
        pl.semaphore_signal(barrier, 1, device_id={"lon": side_lon}, device_id_type=MESH)
    for there, other in ((has_up, lat - 1), (has_down, lat + 1)):
        @pl.when(there)
        def _():
            pl.semaphore_signal(barrier, 1, device_id={"lat": other}, device_id_type=MESH)
            for side_lon in (left, right):
                pl.semaphore_signal(barrier, 1, device_id={"lat": other, "lon": side_lon}, device_id_type=MESH)

    def fill_packs(src):
        for r in range(ROWS):
            pack_r[3 * r : 3 * r + 3, :] = src[r, COLS - MARGIN : COLS, :]
            pack_l[3 * r : 3 * r + 3, :] = src[r, 0:MARGIN, :]

    pack_r[56:64, :] = jnp.zeros((8, channels), f32)
    pack_l[56:64, :] = jnp.zeros((8, channels), f32)
    fill_packs(members_ref)
    pl.semaphore_wait(barrier, n_ens + 1 + 3 * has_up.astype(jnp.int32) + 3 * has_down.astype(jnp.int32))

    def halo_copies(phase, src):
        def remote(k, a, b, to):
            return pltpu.make_async_remote_copy(
                a, b, halo_send.at[phase, k], halo_recv.at[phase, k], device_id=to, device_id_type=MESH
            )

        up, down = lat - 1, lat + 1
        low = pl.ds(0, 16)
        high = pl.ds(48, 16)
        return [
            (None, None, remote(0, pack_r, side.at[phase, 0], {"lon": right})),
            (None, None, remote(1, pack_l, side.at[phase, 1], {"lon": left})),
            (has_down, has_up, remote(2, src.at[pl.ds(ROWS - 3, 3)], updown.at[phase, 0], {"lat": down})),
            (has_up, has_down, remote(3, src.at[pl.ds(0, 3)], updown.at[phase, 1], {"lat": up})),
            (has_down, has_up, remote(4, pack_r.at[high], corner.at[phase, 0], {"lat": down, "lon": right})),
            (has_down, has_up, remote(5, pack_l.at[high], corner.at[phase, 1], {"lat": down, "lon": left})),
            (has_up, has_down, remote(6, pack_r.at[low], corner.at[phase, 2], {"lat": up, "lon": right})),
            (has_up, has_down, remote(7, pack_l.at[low], corner.at[phase, 3], {"lat": up, "lon": left})),
        ]

    def start_halo(phase, src):
        for sends, _, copy in halo_copies(phase, src):
            if sends is None:
                copy.start()
            else:
                pl.when(sends)(copy.start)

    def put_row(r, inner, from_right, from_left):
        hi, lo = split(
            jnp.concatenate([inner, from_right, jnp.zeros((2, channels), f32), from_left], axis=0)
        )
        e_hi[16 * r : 16 * r + 16, :] = hi
        e_lo[16 * r : 16 * r + 16, :] = lo

    def extend(phase, src):
        copies = halo_copies(phase, src)
        for k in (0, 1):
            copies[k][2].wait()
        for r in range(ROWS):
            at = slice(3 * r, 3 * r + 3)
            put_row(r + MARGIN, src[r], side[phase, 1, at, :], side[phase, 0, at, :])
        for there, which, corners, first, offset in (
            (has_up, 0, (0, 1), 0, 3),
            (has_down, 1, (2, 3), ROWS + MARGIN, 0),
        ):
            @pl.when(there)
            def _():
                for k in (2 + which, 4 + 2 * which, 5 + 2 * which):
                    copies[k][2].wait_recv()
                for r in range(3):
                    at = slice(offset + 3 * r, offset + 3 * r + 3)
                    put_row(
                        first + r, updown[phase, which, r],
                        corner[phase, corners[1], at, :], corner[phase, corners[0], at, :],
                    )

            @pl.when(jnp.logical_not(there))
            def _():
                for ref in (e_hi, e_lo):
                    ref[16 * first : 16 * first + 48, :] = jnp.zeros((48, channels), bf16)
        for k in range(2, 8):
            pl.when(copies[k][0])(copies[k][2].wait_send)

    def stencil():
        def one_window(u, carry):
            at = pl.ds(pl.multiple_of(32 * u, 32), 128)
            x_hi, x_lo = e_hi[at, :], e_lo[at, :]
            wh = w_hi[u]
            out = mm(jnp.concatenate([wh, wh], axis=1), jnp.concatenate([x_hi, x_lo], axis=0)) + mm(w_lo[u], x_hi)
            hi, lo = split(out)
            to = pl.ds(pl.multiple_of(16 * u, 16), 16)
            for b in range(BASES):
                s_hi[to, b * channels : (b + 1) * channels] = hi[16 * b : 16 * b + 16]
                s_lo[to, b * channels : (b + 1) * channels] = lo[16 * b : 16 * b + 16]
            return carry

        lax.fori_loop(0, WINDOWS, one_window, 0, unroll=True)

    def mix(cols):
        weights = m_hi[:, cols]
        return mm(s_hi[...], weights) + mm(s_lo[...], weights) + mm(s_hi[...], m_lo[:, cols])

    def chunks():
        return [slice(c, min(c + 256, channels)) for c in range(0, channels, 256)]

    def load_weights(b, carry):
        pltpu.make_async_copy(mixing_ref.at[b], staged.at[b], mix_sem.at[b]).wait()

        def part(k, carry):
            rows = pl.ds(pl.multiple_of(128 * k, 128), 128)
            hi, lo = split(staged[b, rows, :])
            to = pl.ds(pl.multiple_of(b * channels + 128 * k, 128), 128)
            m_hi[to, :] = hi
            m_lo[to, :] = lo
            return carry

        return lax.fori_loop(0, channels // 128, part, carry, unroll=True)

    def transpose_weights(b, carry):
        def part(k, carry):
            cols = pl.ds(pl.multiple_of(128 * k, 128), 128)
            hi, lo = split(staged[b, :, cols].T)
            to = pl.ds(pl.multiple_of(b * channels + 128 * k, 128), 128)
            m_hi[to, :] = hi
            m_lo[to, :] = lo
            return carry

        return lax.fori_loop(0, channels // 128, part, carry, unroll=True)

    start_halo(0, members_ref)
    stencil_matrices(0, stencils_ref, w_hi, w_lo, spaced, by_row)

    zero_piece = jnp.zeros((16, 128), f32)
    a_pack[0, 8 * tiles : 8 * tiles + 16, :] = zero_piece
    truth = jnp.concatenate(
        [analysis_ref[...].reshape(ROWS * COLS, 8 * tiles), jnp.zeros((ROWS * COLS, 128 - 8 * tiles), f32)], axis=1
    )
    main, tail = truth[:128].T, jnp.concatenate([truth[128:], jnp.zeros((96, 128), f32)], axis=0).T
    for t in range(tiles):
        pack_tile(a_pack, main[8 * t : 8 * t + 8], t, 0, 0)
        pack_tile(a_pack, tail[8 * t : 8 * t + 8, 0:32], t, 1, 0)

    lax.fori_loop(0, BASES, load_weights, 0)
    extend(0, members_ref)
    stencil()

    for d in range(n_ens):
        send1[d, 8 * tiles : 8 * tiles + 16, :] = zero_piece
    for cols in chunks():
        width = cols.stop - cols.start
        activation = jnp.tanh(mix(cols))
        damp[:, cols] = 1.0 - activation * activation
        forecast = members_ref[:, :, cols].reshape(ROWS * COLS, width) + activation
        for c in range(width // 128):
            part = forecast[:, 128 * c : 128 * c + 128]
            main = part[:128].T
            tail = jnp.concatenate([part[128:], jnp.zeros((96, 128), f32)], axis=0).T
            for s in range(16):
                k = (cols.start // 128 + c) * 16 + s
                pack_tile(send1, main[8 * s : 8 * s + 8], k % tiles, 0, k // tiles)
                pack_tile(send1, tail[8 * s : 8 * s + 8, 0:32], k % tiles, 1, k // tiles)

    def exchange(phase, src, dst, other, slot):
        return pltpu.make_async_remote_copy(
            src.at[other], dst.at[slot], a2a_send.at[phase, other], a2a_recv.at[phase, slot],
            device_id={"ens": other}, device_id_type=MESH,
        )

    def start_all(phase, src, dst):
        def start(k, carry):
            exchange(phase, src, dst, lax.rem(ens + k, n_ens), ens).start()
            return carry

        lax.fori_loop(1, n_ens, start, 0)
        dst[ens] = src[ens]

    def wait_all(phase, src, dst):
        def wait(k, carry):
            other = lax.rem(ens + k, n_ens)
            exchange(phase, src, dst, other, other).wait_recv()
            exchange(phase, src, dst, other, ens).wait_send()
            return carry

        lax.fori_loop(1, n_ens, wait, 0)

    start_all(0, send1, recv1)
    stencil_matrices(1, stencils_ref, w_hi, w_lo, spaced, by_row)
    lax.fori_loop(0, BASES, transpose_weights, 0)
    wait_all(0, send1, recv1)

    members_total = n_ens
    diagonal = members_total * float(np.sqrt(np.float32(SMOOTH)))
    pairs_scale = 2.0 * members_total * (members_total - 1)

    def score(t, carry):
        rows = pl.ds(pl.multiple_of(8 * t, 8), 8)
        truth = a_pack[0, rows, :]
        x = [recv1[m, rows, :] - truth for m in range(n_ens)]
        slope = [None] * n_ens
        own, pair_abs = None, None
        for m in range(n_ens):
            for n in range(m + 1, n_ens):
                d = x[m] - x[n]
                s2 = d * d + SMOOTH
                r = lax.rsqrt(s2)
                sl = d * r
                ab = s2 * r
                pair_abs = ab if pair_abs is None else pair_abs + ab
                slope[m] = sl if slope[m] is None else slope[m] + sl
                slope[n] = -sl if slope[n] is None else slope[n] - sl
            s2 = x[m] * x[m] + SMOOTH
            r = lax.rsqrt(s2)
            own = s2 * r if own is None else own + s2 * r
            send2[m, rows, :] = x[m] * r - slope[m] * (1.0 / (members_total - 1.0))
        c_pack[0, rows, :] = own * (1.0 / members_total) - (2.0 * pair_abs + diagonal) * (1.0 / pairs_scale)
        return carry

    lax.fori_loop(0, tiles + 2, score, 0)
    start_all(1, send2, recv2)

    main = jnp.concatenate(
        [c_pack[0, 8 * t : 8 * t + 8, :] for t in range(tiles)] + [jnp.zeros((128 - 8 * tiles, 128), f32)], axis=0
    ).T
    crps_ref[0:16] = main[:, 0 : 8 * tiles].reshape(16, COLS, 8 * tiles)
    tail = jnp.concatenate([tail_of(c_pack, t, 0) for t in range(tiles)], axis=0)
    tail = jnp.concatenate([tail, jnp.zeros((8 * tiles, 96), f32)], axis=1)
    tail = jnp.concatenate([tail, jnp.zeros((128 - 8 * tiles, 128), f32)], axis=0).T
    crps_ref[16:20] = tail[0:32, 0 : 8 * tiles].reshape(4, COLS, 8 * tiles)

    wait_all(1, send2, recv2)

    for c in range(channels // 128):
        mains, tails = [], []
        for s in range(16):
            k = c * 16 + s
            piece, t = k // tiles, k % tiles
            mains.append(recv2[piece, 8 * t : 8 * t + 8, :])
            tails.append(tail_of(recv2, t, piece))
        main = jnp.concatenate(mains, axis=0).T
        tail = jnp.concatenate([jnp.concatenate(tails, axis=0), jnp.zeros((128, 96), f32)], axis=1).T
        cols = slice(128 * c, 128 * c + 128)
        grad_ref[0:16, :, cols] = main.reshape(16, COLS, 128)
        grad_ref[16:20, :, cols] = tail[0:32].reshape(4, COLS, 128)
    field[...] = grad_ref[...] * damp[...].reshape(ROWS, COLS, channels)
    fill_packs(field)
    start_halo(1, field)
    extend(1, field)
    stencil()
    for cols in chunks():
        width = cols.stop - cols.start
        grad_ref[:, :, cols] = grad_ref[:, :, cols] + mix(cols).reshape(ROWS, COLS, width)


def local(members, analysis, stencils, mixing):
    channels = members.shape[3]
    n_ens = lax.axis_size("ens")
    per = channels // n_ens
    depth = BASES * channels
    cells = ROWS * COLS
    piece = (n_ens, per + 16, 128)
    vmem = pl.BlockSpec(memory_space=pltpu.VMEM)
    grad, crps = pl.pallas_call(
        step_kernel,
        out_shape=[
            jax.ShapeDtypeStruct((ROWS, COLS, channels), f32),
            jax.ShapeDtypeStruct((ROWS, COLS, per), f32),
        ],
        in_specs=[vmem] * 3 + [pl.BlockSpec(memory_space=pl.ANY)],
        out_specs=[vmem, vmem],
        scratch_shapes=[
            pltpu.VMEM((WINDOWS, 16 * BASES, 128), bf16),
            pltpu.VMEM((WINDOWS, 16 * BASES, 128), bf16),
            pltpu.VMEM((128, 128), f32),
            pltpu.VMEM((128, 128), f32),
            pltpu.VMEM((BASES, channels, channels), f32),
            pltpu.VMEM((depth, channels), bf16),
            pltpu.VMEM((depth, channels), bf16),
            pltpu.VMEM((16 * EXT, channels), bf16),
            pltpu.VMEM((16 * EXT, channels), bf16),
            pltpu.VMEM((cells, depth), bf16),
            pltpu.VMEM((cells, depth), bf16),
            pltpu.VMEM((ROWS, COLS, channels), f32),
            pltpu.VMEM((cells, channels), f32),
            pltpu.VMEM((64, channels), f32),
            pltpu.VMEM((64, channels), f32),
            pltpu.VMEM((2, 2, 64, channels), f32),
            pltpu.VMEM((2, 2, MARGIN, COLS, channels), f32),
            pltpu.VMEM((2, 4, 16, channels), f32),
            pltpu.VMEM((1, per + 16, 128), f32),
            pltpu.VMEM((1, per + 16, 128), f32),
            pltpu.VMEM(piece, f32),
            pltpu.VMEM(piece, f32),
            pltpu.VMEM(piece, f32),
            pltpu.VMEM(piece, f32),
            pltpu.SemaphoreType.DMA((BASES,)),
            pltpu.SemaphoreType.DMA((2, 8)),
            pltpu.SemaphoreType.DMA((2, 8)),
            pltpu.SemaphoreType.DMA((2, n_ens)),
            pltpu.SemaphoreType.DMA((2, n_ens)),
        ],
        compiler_params=pltpu.CompilerParams(
            collective_id=0, has_side_effects=True, vmem_limit_bytes=56 * 1024 * 1024
        ),
        name="ensemble_step",
    )(members[0], analysis, stencils, mixing)
    return grad[None], crps


def solution(mesh):
    in_specs = (P("ens", "lat", "lon", None), P("lat", "lon", "ens"), P(), P())
    out_specs = (P("ens", "lat", "lon", None), P("lat", "lon", "ens"))
    return jax.shard_map(local, mesh=mesh, in_specs=in_specs, out_specs=out_specs, check_vma=False)
```

```python
import functools

import jax
import jax.numpy as jnp
import numpy as np
from jax import lax
from jax.experimental import pallas as pl
from jax.experimental.pallas import tpu as pltpu
from jax.sharding import PartitionSpec as P

BASES = 7
SPAN = 7
MARGIN = 3
ROWS = 20
COLS = 8
WINDOWS = ROWS // 2
EXT = ROWS + 2 * MARGIN
SMOOTH = 0.01
MESH = pl.DeviceIdType.MESH
f32 = jnp.float32
bf16 = jnp.bfloat16


def split(x):
    hi = x.astype(bf16)
    return hi, (x - hi.astype(f32)).astype(bf16)


def mm(a, b):
    return jnp.dot(a, b, preferred_element_type=f32)


def stencil_matrices(kind, st_ref, hi_ref, lo_ref, spaced, by_row):
    lat_rows = st_ref.shape[3]
    first = lax.axis_index("lat") * ROWS
    lane = lax.broadcasted_iota(jnp.int32, (8, 128), 1)
    wrapped = (lane % 16) >= 11
    spaced[...] = jnp.zeros_like(spaced)

    def one_basis(b, carry):
        for p in range(SPAN):
            if kind == 0:
                spaced[16 * p : 16 * p + SPAN, 0:lat_rows] = st_ref[b, p]
            else:
                for q in range(SPAN):
                    r = 16 * p + q
                    spaced[r : r + 1, 0:lat_rows] = st_ref[b, SPAN - 1 - p, SPAN - 1 - q : SPAN - q, :]
        if kind == 0:
            lines = spaced[...]
        else:
            lines = jnp.concatenate(
                [pltpu.roll(spaced[16 * p : 16 * p + 16, :], (MARGIN - p) % 128, 1) for p in range(8)], axis=0
            )
        by_row[...] = pltpu.roll(lines.T, 128 - MARGIN, 1)
        at = pl.ds(pl.multiple_of(16 * b, 16), 16)
        for u in range(WINDOWS):
            rows = []
            for i01 in range(2):
                line = jnp.broadcast_to(by_row[pl.ds(first + 2 * u + i01, 1), :], (8, 128))
                shifted = pltpu.roll(line, 16 * i01, 1, stride=1, stride_axis=0)
                rows.append(jnp.where(wrapped, pltpu.roll(shifted, 16, 1), shifted))
            hi_ref[u, at, :], lo_ref[u, at, :] = split(jnp.concatenate(rows, axis=0))
        return carry

    lax.fori_loop(0, BASES, one_basis, 0)


TILES = 5
BODY = 8 * (TILES + 1)
STEPS = ((0, 1), (2, 3), (4,))
STEP_ROWS = ((0, 24), (24, 16), (40, 8))


def spread_rest(tails, rest):
    for c in range(8):
        lanes = slice(32 * (c % 4), 32 * (c % 4) + 32)
        rest[:, c // 4, lanes] = tails[:, c, 0:32]


def gather_rest(rest, tails):
    for c in range(8):
        lanes = slice(32 * (c % 4), 32 * (c % 4) + 32)
        tails[:, c, 0:32] = rest[:, c // 4, lanes]


def padded(x, rows, lanes):
    if x.shape[1] < lanes:
        x = jnp.concatenate([x, jnp.zeros((x.shape[0], lanes - x.shape[1]), f32)], axis=1)
    if x.shape[0] < rows:
        x = jnp.concatenate([x, jnp.zeros((rows - x.shape[0], lanes), f32)], axis=0)
    return x


def step_kernel(
    members_ref, analysis_ref, stencils_ref, mixing_ref,
    grad_ref, crps_ref,
    w_hi, w_lo, spaced, by_row, staged, turned, m_hi, m_lo, e_hi, e_lo, s_hi, s_lo,
    field, act, damp_main, damp_tail, pack_r, pack_l, side, updown, corner,
    a_body, a_rest, c_body, c_rest, tails, send1, rest1, recv1, got1, send2, rest2, recv2, got2,
    mix_sem, halo_send, halo_recv, a2a_send, a2a_recv,
):
    n_ens = lax.axis_size("ens")
    n_lat = lax.axis_size("lat")
    n_lon = lax.axis_size("lon")
    ens, lat, lon = lax.axis_index("ens"), lax.axis_index("lat"), lax.axis_index("lon")
    right, left = lax.rem(lon + 1, n_lon), lax.rem(lon + n_lon - 1, n_lon)
    has_up, has_down = lat > 0, lat < n_lat - 1
    channels = members_ref.shape[2]
    cells = ROWS * COLS
    per = 8 * TILES

    for b in range(BASES):
        pltpu.make_async_copy(mixing_ref.at[b], staged.at[b], mix_sem.at[b]).start()

    barrier = pltpu.get_barrier_semaphore()

    def greet(k, carry):
        pl.semaphore_signal(barrier, 1, device_id={"ens": lax.rem(ens + k, n_ens)}, device_id_type=MESH)
        return carry

    lax.fori_loop(1, n_ens, greet, 0)
    for side_lon in (left, right):
        pl.semaphore_signal(barrier, 1, device_id={"lon": side_lon}, device_id_type=MESH)
    for there, other in ((has_up, lat - 1), (has_down, lat + 1)):
        @pl.when(there)
        def _():
            pl.semaphore_signal(barrier, 1, device_id={"lat": other}, device_id_type=MESH)
            for side_lon in (left, right):
                pl.semaphore_signal(barrier, 1, device_id={"lat": other, "lon": side_lon}, device_id_type=MESH)

    def fill_packs(src, cols):
        for r in range(ROWS):
            pack_r[3 * r : 3 * r + 3, cols] = src[r, COLS - MARGIN : COLS, cols]
            pack_l[3 * r : 3 * r + 3, cols] = src[r, 0:MARGIN, cols]

    every = slice(0, channels)
    pack_r[56:64, :] = jnp.zeros((8, channels), f32)
    pack_l[56:64, :] = jnp.zeros((8, channels), f32)
    fill_packs(members_ref, every)
    pl.semaphore_wait(barrier, n_ens + 1 + 3 * has_up.astype(jnp.int32) + 3 * has_down.astype(jnp.int32))

    def halo_copies(phase, src, cols):
        back = min(phase, 1)
        lanes = pl.ds(cols.start, cols.stop - cols.start)

        def remote(k, a, b, to):
            return pltpu.make_async_remote_copy(
                a, b, halo_send.at[phase, k], halo_recv.at[phase, k], device_id=to, device_id_type=MESH
            )

        up, down = lat - 1, lat + 1
        low = pl.ds(0, 16)
        high = pl.ds(48, 16)
        return [
            (None, None, remote(0, pack_r.at[:, lanes], side.at[back, 0, :, lanes], {"lon": right})),
            (None, None, remote(1, pack_l.at[:, lanes], side.at[back, 1, :, lanes], {"lon": left})),
            (
                has_down, has_up,
                remote(2, src.at[pl.ds(ROWS - 3, 3), :, lanes], updown.at[back, 0, :, :, lanes], {"lat": down}),
            ),
            (
                has_up, has_down,
                remote(3, src.at[pl.ds(0, 3), :, lanes], updown.at[back, 1, :, :, lanes], {"lat": up}),
            ),
            (
                has_down, has_up,
                remote(4, pack_r.at[high, lanes], corner.at[back, 0, :, lanes], {"lat": down, "lon": right}),
            ),
            (
                has_down, has_up,
                remote(5, pack_l.at[high, lanes], corner.at[back, 1, :, lanes], {"lat": down, "lon": left}),
            ),
            (
                has_up, has_down,
                remote(6, pack_r.at[low, lanes], corner.at[back, 2, :, lanes], {"lat": up, "lon": right}),
            ),
            (
                has_up, has_down,
                remote(7, pack_l.at[low, lanes], corner.at[back, 3, :, lanes], {"lat": up, "lon": left}),
            ),
        ]

    def start_halo(phase, src, cols):
        for sends, _, copy in halo_copies(phase, src, cols):
            if sends is None:
                copy.start()
            else:
                pl.when(sends)(copy.start)

    def put_row(r, inner, from_right, from_left, cols):
        gap = jnp.zeros((2, cols.stop - cols.start), f32)
        hi, lo = split(jnp.concatenate([inner, from_right, gap, from_left], axis=0))
        e_hi[16 * r : 16 * r + 16, cols] = hi
        e_lo[16 * r : 16 * r + 16, cols] = lo

    def extend(phase, src, cols):
        copies = halo_copies(phase, src, cols)
        back = min(phase, 1)
        for k in (0, 1):
            copies[k][2].wait()
        for r in range(ROWS):
            at = slice(3 * r, 3 * r + 3)
            put_row(r + MARGIN, src[r, :, cols], side[back, 1, at, cols], side[back, 0, at, cols], cols)
        for there, which, corners, first, offset in (
            (has_up, 0, (0, 1), 0, 3),
            (has_down, 1, (2, 3), ROWS + MARGIN, 0),
        ):
            @pl.when(there)
            def _():
                for k in (2 + which, 4 + 2 * which, 5 + 2 * which):
                    copies[k][2].wait_recv()
                for r in range(3):
                    at = slice(offset + 3 * r, offset + 3 * r + 3)
                    put_row(
                        first + r, updown[back, which, r, :, cols],
                        corner[back, corners[1], at, cols], corner[back, corners[0], at, cols], cols,
                    )

            @pl.when(jnp.logical_not(there))
            def _():
                for ref in (e_hi, e_lo):
                    ref[16 * first : 16 * first + 48, cols] = jnp.zeros((48, cols.stop - cols.start), bf16)
        for k in range(2, 8):
            pl.when(copies[k][0])(copies[k][2].wait_send)

    def stencil(cols):
        width = cols.stop - cols.start

        def one_window(u, carry):
            at = pl.ds(pl.multiple_of(32 * u, 32), 128)
            x_hi, x_lo = e_hi[at, cols], e_lo[at, cols]
            wh = w_hi[u]
            out = mm(jnp.concatenate([wh, wh], axis=1), jnp.concatenate([x_hi, x_lo], axis=0)) + mm(w_lo[u], x_hi)
            hi, lo = split(out)
            to = pl.ds(pl.multiple_of(16 * u, 16), 16)
            for b in range(BASES):
                here = slice(BASES * cols.start + b * width, BASES * cols.start + (b + 1) * width)
                s_hi[to, here] = hi[16 * b : 16 * b + 16]
                s_lo[to, here] = lo[16 * b : 16 * b + 16]
            return carry

        lax.fori_loop(0, WINDOWS, one_window, 0, unroll=True)

    def mix(cols, inputs):
        k = slice(BASES * inputs.start, BASES * inputs.stop)
        weights = m_hi[k, cols]
        return mm(s_hi[:, k], weights) + mm(s_lo[:, k], weights) + mm(s_hi[:, k], m_lo[k, cols])

    def chunks():
        return [slice(c, min(c + 256, channels)) for c in range(0, channels, 256)]

    def load_weights(b, carry):
        pltpu.make_async_copy(mixing_ref.at[b], staged.at[b], mix_sem.at[b]).wait()
        for k in range(channels // 128):
            hi, lo = split(staged[b, 128 * k : 128 * k + 128, :])
            to = pl.ds(pl.multiple_of(b * channels + 128 * k, 128), 128)
            m_hi[to, :] = hi
            m_lo[to, :] = lo
        return carry

    def transpose_weights(b, carry):
        for k in range(channels // 128):
            turned[128 * k : 128 * k + 128, :] = staged[b, :, 128 * k : 128 * k + 128].T
        for first, tiles in ((128 * step[0], step) for step in STEPS):
            width = 128 * len(tiles)
            for n, j in enumerate(tiles):
                for d in range(0, n_ens, 2):
                    low, high = 8 * (TILES * d + j), 8 * (TILES * (d + 1) + j)
                    hi, lo = split(jnp.concatenate([turned[low : low + 8, :], turned[high : high + 8, :]], axis=0))
                    to = pl.ds(pl.multiple_of(BASES * first + b * width + 128 * n + 8 * d, 16), 16)
                    m_hi[to, :] = hi
                    m_lo[to, :] = lo
        return carry

    start_halo(0, members_ref, every)
    stencil_matrices(0, stencils_ref, w_hi, w_lo, spaced, by_row)

    truth = padded(analysis_ref[...].reshape(cells, per), cells, 128)
    main, tail = truth[:128].T, padded(truth[128:], 128, 128).T
    for j in range(TILES):
        a_body[8 + 8 * j : 16 + 8 * j, :] = main[8 * j : 8 * j + 8]
        if j < 4:
            a_body[0:8, 32 * j : 32 * j + 32] = tail[8 * j : 8 * j + 8, 0:32]
        else:
            for c in range(8):
                a_rest[c // 4 : c // 4 + 1, 32 * (c % 4) : 32 * (c % 4) + 32] = tail[8 * j + c : 8 * j + c + 1, 0:32]

    lax.fori_loop(0, BASES, load_weights, 0)
    extend(0, members_ref, every)
    stencil(every)

    def body_copy(phase, step, src, dst, other, slot):
        first, count = STEP_ROWS[step]
        rows = pl.ds(first, count)
        return pltpu.make_async_remote_copy(
            src.at[other, rows], dst.at[slot, rows], a2a_send.at[phase, step, other], a2a_recv.at[phase, step, slot],
            device_id={"ens": other}, device_id_type=MESH,
        )

    def rest_copy(phase, src, dst, other, slot):
        return pltpu.make_async_remote_copy(
            src.at[other], dst.at[slot], a2a_send.at[phase, 3, other], a2a_recv.at[phase, 3, slot],
            device_id={"ens": other}, device_id_type=MESH,
        )

    def peers(action):
        def one(k, carry):
            action(lax.rem(ens + k, n_ens))
            return carry

        lax.fori_loop(1, n_ens, one, 0)

    done = 0
    for cols in chunks():
        width = cols.stop - cols.start
        activation = jnp.tanh(mix(cols, every))
        act[:, cols] = activation
        forecast = members_ref[:, :, cols].reshape(cells, width) + activation
        for c in range(width // 128):
            part = forecast[:, 128 * c : 128 * c + 128]
            main, tail = part[:128].T, padded(part[128:], 128, 128).T
            for n in range(16):
                k = (cols.start // 128 + c) * 16 + n
                d, j = k // TILES, k % TILES
                send1[d, 8 + 8 * j : 16 + 8 * j, :] = main[8 * n : 8 * n + 8]
                if j < 4:
                    send1[d, 0:8, 32 * j : 32 * j + 32] = tail[8 * n : 8 * n + 8, 0:32]
                else:
                    tails[d, :, 0:32] = tail[8 * n : 8 * n + 8, 0:32]
        for d in range(done, cols.stop // per):
            pl.when(ens != d)(body_copy(0, 0, send1, recv1, d, ens).start)
        done = cols.stop // per
    spread_rest(tails, rest1)
    peers(lambda other: rest_copy(0, rest1, got1, other, ens).start())
    for step in (1, 2):
        peers(lambda other: body_copy(0, step, send1, recv1, other, ens).start())
    recv1[ens] = send1[ens]
    got1[ens] = rest1[ens]

    lax.fori_loop(0, BASES, transpose_weights, 0)
    for c in range(channels // 128):
        damp = act[:, 128 * c : 128 * c + 128]
        damp = 1.0 - damp * damp
        damp_main[128 * c : 128 * c + 128, :] = damp[:128].T
        damp_tail[128 * c : 128 * c + 128, :] = padded(damp[128:], 128, 128).T

    members_total = n_ens
    diagonal = members_total * float(np.sqrt(np.float32(SMOOTH)))
    pairs_scale = 2.0 * members_total * (members_total - 1)

    def score(read, truth, write):
        x = [read(m) - truth for m in range(n_ens)]
        slope = [None] * n_ens
        own, pair_abs = None, None
        for m in range(n_ens):
            for n in range(m + 1, n_ens):
                d = x[m] - x[n]
                s2 = d * d + SMOOTH
                r = lax.rsqrt(s2)
                sl = d * r
                ab = s2 * r
                pair_abs = ab if pair_abs is None else pair_abs + ab
                slope[m] = sl if slope[m] is None else slope[m] + sl
                slope[n] = -sl if slope[n] is None else slope[n] - sl
            s2 = x[m] * x[m] + SMOOTH
            r = lax.rsqrt(s2)
            own = s2 * r if own is None else own + s2 * r
            write(m, x[m] * r - slope[m] * (1.0 / (members_total - 1.0)))
        return own * (1.0 / members_total) - (2.0 * pair_abs + diagonal) * (1.0 / pairs_scale)

    def score_rows(t, carry):
        rows = pl.ds(pl.multiple_of(8 * t, 8), 8)

        def write(m, value):
            send2[m, rows, :] = value

        c_body[rows, :] = score(lambda m: recv1[m, rows, :], a_body[rows, :], write)
        return carry

    def score_rest():
        def write(m, value):
            rest2[m] = value

        c_rest[...] = score(lambda m: got1[m], a_rest[...], write)

    for step in range(3):
        peers(lambda other: body_copy(0, step, send1, recv1, other, other).wait_recv())
        first, count = STEP_ROWS[step]
        lax.fori_loop(first // 8, (first + count) // 8, score_rows, 0)
        peers(lambda other: body_copy(1, step, send2, recv2, other, ens).start())
        if step == 0:
            peers(lambda other: rest_copy(0, rest1, got1, other, other).wait_recv())
            score_rest()
            peers(lambda other: rest_copy(1, rest2, got2, other, ens).start())
            stencil_matrices(1, stencils_ref, w_hi, w_lo, spaced, by_row)
    recv2[ens] = send2[ens]
    got2[ens] = rest2[ens]

    mains = [c_body[8 + 8 * j : 16 + 8 * j, :] for j in range(TILES)]
    parts = [c_body[0:8, 32 * j : 32 * j + 32] for j in range(4)]
    parts += [c_rest[c // 4 : c // 4 + 1, 32 * (c % 4) : 32 * (c % 4) + 32] for c in range(8)]
    main = padded(jnp.concatenate(mains, axis=0), 128, 128).T
    tail = padded(jnp.concatenate(parts, axis=0), 128, 128).T
    crps_ref[0:16] = main[:, 0:per].reshape(16, COLS, per)
    crps_ref[16:20] = tail[0:32, 0:per].reshape(4, COLS, per)

    def tile_tail(d, j):
        return recv2[d, 0:8, 32 * j : 32 * j + 32] if j < 4 else tails[d, :, 0:32]

    def returned(step):
        peers(lambda other: body_copy(1, step, send2, recv2, other, other).wait_recv())
        if step == 0:
            peers(lambda other: rest_copy(1, rest2, got2, other, other).wait_recv())
            gather_rest(got2, tails)
        for j in STEPS[step]:
            mains, parts = [], []
            for d in range(n_ens):
                at = slice(8 * (TILES * d + j), 8 * (TILES * d + j) + 8)
                mains.append(recv2[d, 8 + 8 * j : 16 + 8 * j, :] * damp_main[at, :])
                parts.append(tile_tail(d, j) * damp_tail[at, 0:32])
            main = jnp.concatenate(mains, axis=0).T
            tail = padded(jnp.concatenate(parts, axis=0), 128, 128).T
            cols = slice(128 * j, 128 * j + 128)
            field[0:16, :, cols] = main.reshape(16, COLS, 128)
            field[16:20, :, cols] = tail[0:32].reshape(4, COLS, 128)
        cols = slice(128 * STEPS[step][0], 128 * STEPS[step][-1] + 128)
        fill_packs(field, cols)
        start_halo(1 + step, field, cols)

    def adjoint(step):
        inputs = slice(128 * STEPS[step][0], 128 * STEPS[step][-1] + 128)
        extend(1 + step, field, inputs)
        stencil(inputs)
        for cols in chunks():
            more = mix(cols, inputs).reshape(ROWS, COLS, cols.stop - cols.start)
            grad_ref[:, :, cols] = more if step == 0 else grad_ref[:, :, cols] + more

    returned(0)
    returned(1)
    adjoint(0)
    returned(2)
    adjoint(1)
    for c in range(channels // 128):
        mains, parts = [], []
        for n in range(16):
            k = 16 * c + n
            d, j = k // TILES, k % TILES
            mains.append(recv2[d, 8 + 8 * j : 16 + 8 * j, :])
            parts.append(tile_tail(d, j))
        main = jnp.concatenate(mains, axis=0).T
        tail = padded(jnp.concatenate(parts, axis=0), 128, 128).T
        cols = slice(128 * c, 128 * c + 128)
        grad_ref[0:16, :, cols] = grad_ref[0:16, :, cols] + main.reshape(16, COLS, 128)
        grad_ref[16:20, :, cols] = grad_ref[16:20, :, cols] + tail[0:32].reshape(4, COLS, 128)
    adjoint(2)

    for phase, body, rest, there, got in ((0, send1, rest1, recv1, got1), (1, send2, rest2, recv2, got2)):
        for step in range(3):
            peers(lambda other: body_copy(phase, step, body, there, other, ens).wait_send())
        peers(lambda other: rest_copy(phase, rest, got, other, ens).wait_send())


def local(members, analysis, stencils, mixing):
    channels = members.shape[3]
    n_ens = lax.axis_size("ens")
    per = channels // n_ens
    depth = BASES * channels
    cells = ROWS * COLS
    vmem = pl.BlockSpec(memory_space=pltpu.VMEM)
    body = pltpu.VMEM((n_ens, BODY, 128), f32)
    rest = pltpu.VMEM((n_ens, 2, 128), f32)
    grad, crps = pl.pallas_call(
        step_kernel,
        out_shape=[
            jax.ShapeDtypeStruct((ROWS, COLS, channels), f32),
            jax.ShapeDtypeStruct((ROWS, COLS, per), f32),
        ],
        in_specs=[vmem] * 3 + [pl.BlockSpec(memory_space=pl.ANY)],
        out_specs=[vmem, vmem],
        scratch_shapes=[
            pltpu.VMEM((WINDOWS, 16 * BASES, 128), bf16),
            pltpu.VMEM((WINDOWS, 16 * BASES, 128), bf16),
            pltpu.VMEM((128, 128), f32),
            pltpu.VMEM((128, 128), f32),
            pltpu.VMEM((BASES, channels, channels), f32),
            pltpu.VMEM((channels, channels), f32),
            pltpu.VMEM((depth, channels), bf16),
            pltpu.VMEM((depth, channels), bf16),
            pltpu.VMEM((16 * EXT, channels), bf16),
            pltpu.VMEM((16 * EXT, channels), bf16),
            pltpu.VMEM((cells, depth), bf16),
            pltpu.VMEM((cells, depth), bf16),
            pltpu.VMEM((ROWS, COLS, channels), f32),
            pltpu.VMEM((cells, channels), f32),
            pltpu.VMEM((channels, 128), f32),
            pltpu.VMEM((channels, 128), f32),
            pltpu.VMEM((64, channels), f32),
            pltpu.VMEM((64, channels), f32),
            pltpu.VMEM((2, 2, 64, channels), f32),
            pltpu.VMEM((2, 2, MARGIN, COLS, channels), f32),
            pltpu.VMEM((2, 4, 16, channels), f32),
            pltpu.VMEM((BODY, 128), f32),
            pltpu.VMEM((2, 128), f32),
            pltpu.VMEM((BODY, 128), f32),
            pltpu.VMEM((2, 128), f32),
            pltpu.VMEM((n_ens, 8, 128), f32),
            body, rest, body, rest,
            body, rest, body, rest,
            pltpu.SemaphoreType.DMA((BASES,)),
            pltpu.SemaphoreType.DMA((4, 8)),
            pltpu.SemaphoreType.DMA((4, 8)),
            pltpu.SemaphoreType.DMA((2, 4, n_ens)),
            pltpu.SemaphoreType.DMA((2, 4, n_ens)),
        ],
        compiler_params=pltpu.CompilerParams(
            collective_id=0, has_side_effects=True, vmem_limit_bytes=56 * 1024 * 1024
        ),
        name="ensemble_step",
    )(members[0], analysis, stencils, mixing)
    return grad[None], crps


def solution(mesh):
    in_specs = (P("ens", "lat", "lon", None), P("lat", "lon", "ens"), P(), P())
    out_specs = (P("ens", "lat", "lon", None), P("lat", "lon", "ens"))
    return jax.shard_map(local, mesh=mesh, in_specs=in_specs, out_specs=out_specs, check_vma=False)
```

```python
import functools

import jax
import jax.numpy as jnp
import numpy as np
from jax import lax
from jax.experimental import pallas as pl
from jax.experimental.pallas import tpu as pltpu
from jax.sharding import PartitionSpec as P

BASES = 7
SPAN = 7
MARGIN = 3
ROWS = 20
COLS = 8
WINDOWS = ROWS // 2
EXT = ROWS + 2 * MARGIN
SMOOTH = 0.01
MESH = pl.DeviceIdType.MESH
f32 = jnp.float32
bf16 = jnp.bfloat16


def split(x):
    hi = x.astype(bf16)
    return hi, (x - hi.astype(f32)).astype(bf16)


def mm(a, b):
    return jnp.dot(a, b, preferred_element_type=f32)


def stencil_matrices(kind, st_ref, hi_ref, lo_ref, spaced, by_row):
    lat_rows = st_ref.shape[3]
    first = lax.axis_index("lat") * ROWS
    lane = lax.broadcasted_iota(jnp.int32, (8, 128), 1)
    wrapped = (lane % 16) >= 11
    spaced[...] = jnp.zeros_like(spaced)

    def one_basis(b, carry):
        for p in range(SPAN):
            if kind == 0:
                spaced[16 * p : 16 * p + SPAN, 0:lat_rows] = st_ref[b, p]
            else:
                for q in range(SPAN):
                    r = 16 * p + q
                    spaced[r : r + 1, 0:lat_rows] = st_ref[b, SPAN - 1 - p, SPAN - 1 - q : SPAN - q, :]
        if kind == 0:
            lines = spaced[...]
        else:
            lines = jnp.concatenate(
                [pltpu.roll(spaced[16 * p : 16 * p + 16, :], (MARGIN - p) % 128, 1) for p in range(8)], axis=0
            )
        by_row[...] = pltpu.roll(lines.T, 128 - MARGIN, 1)
        at = pl.ds(pl.multiple_of(16 * b, 16), 16)
        for u in range(WINDOWS):
            rows = []
            for i01 in range(2):
                line = jnp.broadcast_to(by_row[pl.ds(first + 2 * u + i01, 1), :], (8, 128))
                shifted = pltpu.roll(line, 16 * i01, 1, stride=1, stride_axis=0)
                rows.append(jnp.where(wrapped, pltpu.roll(shifted, 16, 1), shifted))
            hi_ref[u, at, :], lo_ref[u, at, :] = split(jnp.concatenate(rows, axis=0))
        return carry

    lax.fori_loop(0, BASES, one_basis, 0)


TILES = 5
BODY = 8 * (TILES + 1)
STEPS = ((0, 1), (2, 3), (4,))
STEP_ROWS = ((0, 24), (24, 16), (40, 8))


def spread_rest(tails, rest):
    for c in range(8):
        lanes = slice(32 * (c % 4), 32 * (c % 4) + 32)
        rest[:, c // 4, lanes] = tails[:, c, 0:32]


def gather_rest(rest, tails):
    for c in range(8):
        lanes = slice(32 * (c % 4), 32 * (c % 4) + 32)
        tails[:, c, 0:32] = rest[:, c // 4, lanes]


def padded(x, rows, lanes):
    if x.shape[1] < lanes:
        x = jnp.concatenate([x, jnp.zeros((x.shape[0], lanes - x.shape[1]), f32)], axis=1)
    if x.shape[0] < rows:
        x = jnp.concatenate([x, jnp.zeros((rows - x.shape[0], lanes), f32)], axis=0)
    return x


def step_kernel(
    members_hbm, analysis_hbm, stencils_hbm, mixing_ref,
    grad_ref, crps_ref,
    members_ref, analysis_ref, stencils_ref, in_sem,
    w_hi, w_lo, spaced, by_row, staged, turned, m_hi, m_lo, e_hi, e_lo, s_hi, s_lo,
    field, act, damp_main, damp_tail, pack_r, pack_l, side, updown, corner,
    a_body, a_rest, c_body, c_rest, tails, send1, rest1, recv1, got1, send2, rest2, recv2, got2,
    mix_sem, halo_send, halo_recv, a2a_send, a2a_recv,
):
    n_ens = lax.axis_size("ens")
    n_lat = lax.axis_size("lat")
    n_lon = lax.axis_size("lon")
    ens, lat, lon = lax.axis_index("ens"), lax.axis_index("lat"), lax.axis_index("lon")
    right, left = lax.rem(lon + 1, n_lon), lax.rem(lon + n_lon - 1, n_lon)
    has_up, has_down = lat > 0, lat < n_lat - 1
    channels = members_hbm.shape[2]
    cells = ROWS * COLS
    per = 8 * TILES

    def chunks():
        return [slice(c, min(c + 256, channels)) for c in range(0, channels, 256)]

    loads = [
        pltpu.make_async_copy(src, dst, in_sem.at[k])
        for k, (src, dst) in enumerate(
            ((members_hbm, members_ref), (stencils_hbm, stencils_ref), (analysis_hbm, analysis_ref))
        )
    ]
    for load in loads:
        load.start()

    def weights_copy(n, cols):
        rows = pl.ds(cols.start, cols.stop - cols.start)
        return pltpu.make_async_copy(mixing_ref.at[:, rows], staged.at[:, rows], mix_sem.at[n])

    for n, cols in enumerate(chunks()):
        weights_copy(n, cols).start()

    barrier = pltpu.get_barrier_semaphore()

    def greet(k, carry):
        pl.semaphore_signal(barrier, 1, device_id={"ens": lax.rem(ens + k, n_ens)}, device_id_type=MESH)
        return carry

    lax.fori_loop(1, n_ens, greet, 0)
    for side_lon in (left, right):
        pl.semaphore_signal(barrier, 1, device_id={"lon": side_lon}, device_id_type=MESH)
    for there, other in ((has_up, lat - 1), (has_down, lat + 1)):
        @pl.when(there)
        def _():
            pl.semaphore_signal(barrier, 1, device_id={"lat": other}, device_id_type=MESH)
            for side_lon in (left, right):
                pl.semaphore_signal(barrier, 1, device_id={"lat": other, "lon": side_lon}, device_id_type=MESH)

    def fill_packs(src, cols):
        for r in range(ROWS):
            pack_r[3 * r : 3 * r + 3, cols] = src[r, COLS - MARGIN : COLS, cols]
            pack_l[3 * r : 3 * r + 3, cols] = src[r, 0:MARGIN, cols]

    every = slice(0, channels)
    pack_r[56:64, :] = jnp.zeros((8, channels), f32)
    pack_l[56:64, :] = jnp.zeros((8, channels), f32)
    for load in loads:
        load.wait()
    fill_packs(members_ref, every)
    pl.semaphore_wait(barrier, n_ens + 1 + 3 * has_up.astype(jnp.int32) + 3 * has_down.astype(jnp.int32))

    def halo_copies(phase, src, cols):
        back = phase // 3
        lanes = pl.ds(cols.start, cols.stop - cols.start)

        def remote(k, a, b, to):
            return pltpu.make_async_remote_copy(
                a, b, halo_send.at[phase, k], halo_recv.at[phase, k], device_id=to, device_id_type=MESH
            )

        up, down = lat - 1, lat + 1
        low = pl.ds(0, 16)
        high = pl.ds(48, 16)
        return [
            (None, None, remote(0, pack_r.at[:, lanes], side.at[back, 0, :, lanes], {"lon": right})),
            (None, None, remote(1, pack_l.at[:, lanes], side.at[back, 1, :, lanes], {"lon": left})),
            (
                has_down, has_up,
                remote(2, src.at[pl.ds(ROWS - 3, 3), :, lanes], updown.at[back, 0, :, :, lanes], {"lat": down}),
            ),
            (
                has_up, has_down,
                remote(3, src.at[pl.ds(0, 3), :, lanes], updown.at[back, 1, :, :, lanes], {"lat": up}),
            ),
            (
                has_down, has_up,
                remote(4, pack_r.at[high, lanes], corner.at[back, 0, :, lanes], {"lat": down, "lon": right}),
            ),
            (
                has_down, has_up,
                remote(5, pack_l.at[high, lanes], corner.at[back, 1, :, lanes], {"lat": down, "lon": left}),
            ),
            (
                has_up, has_down,
                remote(6, pack_r.at[low, lanes], corner.at[back, 2, :, lanes], {"lat": up, "lon": right}),
            ),
            (
                has_up, has_down,
                remote(7, pack_l.at[low, lanes], corner.at[back, 3, :, lanes], {"lat": up, "lon": left}),
            ),
        ]

    def start_halo(phase, src, cols):
        for sends, _, copy in halo_copies(phase, src, cols):
            if sends is None:
                copy.start()
            else:
                pl.when(sends)(copy.start)

    def put_row(r, inner, from_right, from_left, cols):
        gap = jnp.zeros((2, cols.stop - cols.start), f32)
        hi, lo = split(jnp.concatenate([inner, from_right, gap, from_left], axis=0))
        e_hi[16 * r : 16 * r + 16, cols] = hi
        e_lo[16 * r : 16 * r + 16, cols] = lo

    def extend(phase, src, cols):
        copies = halo_copies(phase, src, cols)
        back = phase // 3
        for k in (0, 1):
            copies[k][2].wait_recv()
        for r in range(ROWS):
            at = slice(3 * r, 3 * r + 3)
            put_row(r + MARGIN, src[r, :, cols], side[back, 1, at, cols], side[back, 0, at, cols], cols)
        for there, which, corners, first, offset in (
            (has_up, 0, (0, 1), 0, 3),
            (has_down, 1, (2, 3), ROWS + MARGIN, 0),
        ):
            @pl.when(there)
            def _():
                for k in (2 + which, 4 + 2 * which, 5 + 2 * which):
                    copies[k][2].wait_recv()
                for r in range(3):
                    at = slice(offset + 3 * r, offset + 3 * r + 3)
                    put_row(
                        first + r, updown[back, which, r, :, cols],
                        corner[back, corners[1], at, cols], corner[back, corners[0], at, cols], cols,
                    )

            @pl.when(jnp.logical_not(there))
            def _():
                for ref in (e_hi, e_lo):
                    ref[16 * first : 16 * first + 48, cols] = jnp.zeros((48, cols.stop - cols.start), bf16)

    def halo_sent(phase, src, cols):
        for sends, _, copy in halo_copies(phase, src, cols):
            if sends is None:
                copy.wait_send()
            else:
                pl.when(sends)(copy.wait_send)

    def stencil(cols):
        width = cols.stop - cols.start

        def one_window(u, carry):
            at = pl.ds(pl.multiple_of(32 * u, 32), 128)
            x_hi, x_lo = e_hi[at, cols], e_lo[at, cols]
            wh = w_hi[u]
            out = mm(jnp.concatenate([wh, wh], axis=1), jnp.concatenate([x_hi, x_lo], axis=0)) + mm(w_lo[u], x_hi)
            hi, lo = split(out)
            to = pl.ds(pl.multiple_of(16 * u, 16), 16)
            for b in range(BASES):
                here = slice(BASES * cols.start + b * width, BASES * cols.start + (b + 1) * width)
                s_hi[to, here] = hi[16 * b : 16 * b + 16]
                s_lo[to, here] = lo[16 * b : 16 * b + 16]
            return carry

        lax.fori_loop(0, WINDOWS, one_window, 0, unroll=True)

    def mix(cols, inputs):
        k = slice(BASES * inputs.start, BASES * inputs.stop)
        weights, more = m_hi[k, cols], m_lo[k, cols]
        width = cols.stop - cols.start
        if width == 128:
            both = mm(s_hi[:, k], jnp.concatenate([weights, more], axis=1))
            return both[:, :128] + both[:, 128:] + mm(s_lo[:, k], weights)
        return mm(s_hi[:, k], weights) + mm(s_lo[:, k], weights) + mm(s_hi[:, k], more)

    def load_weights(n, cols):
        weights_copy(n, cols).wait()
        width = cols.stop - cols.start

        def one_basis(b, carry):
            for k in range(width // 128):
                at = cols.start + 128 * k
                hi, lo = split(staged[b, at : at + 128, :])
                to = pl.ds(pl.multiple_of(BASES * cols.start + b * width + 128 * k, 128), 128)
                m_hi[to, :] = hi
                m_lo[to, :] = lo
            return carry

        lax.fori_loop(0, BASES, one_basis, 0)

    def transpose_weights(b, carry):
        for k in range(channels // 128):
            turned[128 * k : 128 * k + 128, :] = staged[b, :, 128 * k : 128 * k + 128].T
        for first, tiles in ((128 * step[0], step) for step in STEPS):
            width = 128 * len(tiles)
            for n, j in enumerate(tiles):
                for d in range(0, n_ens, 2):
                    low, high = 8 * (TILES * d + j), 8 * (TILES * (d + 1) + j)
                    hi, lo = split(jnp.concatenate([turned[low : low + 8, :], turned[high : high + 8, :]], axis=0))
                    to = pl.ds(pl.multiple_of(BASES * first + b * width + 128 * n + 8 * d, 16), 16)
                    m_hi[to, :] = hi
                    m_lo[to, :] = lo
        return carry

    for n, cols in enumerate(chunks()):
        start_halo(n, members_ref, cols)
    stencil_matrices(0, stencils_ref, w_hi, w_lo, spaced, by_row)

    for n, inputs in enumerate(chunks()):
        load_weights(n, inputs)
        extend(n, members_ref, inputs)
        stencil(inputs)

    def body_copy(phase, step, src, dst, other, slot):
        first, count = STEP_ROWS[step]
        rows = pl.ds(first, count)
        return pltpu.make_async_remote_copy(
            src.at[other, rows], dst.at[slot, rows], a2a_send.at[phase, step, other], a2a_recv.at[phase, step, slot],
            device_id={"ens": other}, device_id_type=MESH,
        )

    def rest_copy(phase, src, dst, other, slot):
        return pltpu.make_async_remote_copy(
            src.at[other], dst.at[slot], a2a_send.at[phase, 3, other], a2a_recv.at[phase, 3, slot],
            device_id={"ens": other}, device_id_type=MESH,
        )

    def peers(action):
        def one(k, carry):
            action(lax.rem(ens + k, n_ens))
            return carry

        lax.fori_loop(1, n_ens, one, 0)

    done = 0
    for cols in chunks():
        width = cols.stop - cols.start
        activation = jnp.tanh(mix(cols, every))
        act[:, cols] = activation
        forecast = members_ref[:, :, cols].reshape(cells, width) + activation
        for c in range(width // 128):
            part = forecast[:, 128 * c : 128 * c + 128]
            main, tail = part[:128].T, padded(part[128:], 128, 128).T
            for n in range(16):
                k = (cols.start // 128 + c) * 16 + n
                d, j = k // TILES, k % TILES
                send1[d, 8 + 8 * j : 16 + 8 * j, :] = main[8 * n : 8 * n + 8]
                if j < 4:
                    send1[d, 0:8, 32 * j : 32 * j + 32] = tail[8 * n : 8 * n + 8, 0:32]
                else:
                    tails[d, :, 0:32] = tail[8 * n : 8 * n + 8, 0:32]
        for d in range(done, cols.stop // per):
            pl.when(ens != d)(body_copy(0, 0, send1, recv1, d, ens).start)
        done = cols.stop // per
    spread_rest(tails, rest1)
    peers(lambda other: rest_copy(0, rest1, got1, other, ens).start())
    for step in (1, 2):
        peers(lambda other: body_copy(0, step, send1, recv1, other, ens).start())
    recv1[ens] = send1[ens]
    got1[ens] = rest1[ens]

    for n, cols in enumerate(chunks()):
        halo_sent(n, members_ref, cols)

    truth = padded(analysis_ref[...].reshape(cells, per), cells, 128)
    main, tail = truth[:128].T, padded(truth[128:], 128, 128).T
    for j in range(TILES):
        a_body[8 + 8 * j : 16 + 8 * j, :] = main[8 * j : 8 * j + 8]
        if j < 4:
            a_body[0:8, 32 * j : 32 * j + 32] = tail[8 * j : 8 * j + 8, 0:32]
        else:
            for c in range(8):
                a_rest[c // 4 : c // 4 + 1, 32 * (c % 4) : 32 * (c % 4) + 32] = tail[8 * j + c : 8 * j + c + 1, 0:32]

    lax.fori_loop(0, BASES, transpose_weights, 0)
    for c in range(channels // 128):
        damp = act[:, 128 * c : 128 * c + 128]
        damp = 1.0 - damp * damp
        damp_main[128 * c : 128 * c + 128, :] = damp[:128].T
        damp_tail[128 * c : 128 * c + 128, :] = padded(damp[128:], 128, 128).T

    members_total = n_ens
    diagonal = members_total * float(np.sqrt(np.float32(SMOOTH)))
    pairs_scale = 2.0 * members_total * (members_total - 1)

    def score(read, truth, write):
        x = [read(m) - truth for m in range(n_ens)]
        slope = [None] * n_ens
        own, pair_abs = None, None
        for m in range(n_ens):
            for n in range(m + 1, n_ens):
                d = x[m] - x[n]
                s2 = d * d + SMOOTH
                r = lax.rsqrt(s2)
                sl = d * r
                ab = s2 * r
                pair_abs = ab if pair_abs is None else pair_abs + ab
                slope[m] = sl if slope[m] is None else slope[m] + sl
                slope[n] = -sl if slope[n] is None else slope[n] - sl
            s2 = x[m] * x[m] + SMOOTH
            r = lax.rsqrt(s2)
            own = s2 * r if own is None else own + s2 * r
            write(m, x[m] * r - slope[m] * (1.0 / (members_total - 1.0)))
        return own * (1.0 / members_total) - (2.0 * pair_abs + diagonal) * (1.0 / pairs_scale)

    def score_rows(t, carry):
        rows = pl.ds(pl.multiple_of(8 * t, 8), 8)

        def write(m, value):
            send2[m, rows, :] = value

        c_body[rows, :] = score(lambda m: recv1[m, rows, :], a_body[rows, :], write)
        return carry

    def score_rest():
        def write(m, value):
            rest2[m] = value

        c_rest[...] = score(lambda m: got1[m], a_rest[...], write)

    for step in range(3):
        peers(lambda other: body_copy(0, step, send1, recv1, other, other).wait_recv())
        first, count = STEP_ROWS[step]
        lax.fori_loop(first // 8, (first + count) // 8, score_rows, 0)
        peers(lambda other: body_copy(1, step, send2, recv2, other, ens).start())
        if step == 0:
            peers(lambda other: rest_copy(0, rest1, got1, other, other).wait_recv())
            score_rest()
            peers(lambda other: rest_copy(1, rest2, got2, other, ens).start())
    recv2[ens] = send2[ens]
    got2[ens] = rest2[ens]
    stencil_matrices(1, stencils_ref, w_hi, w_lo, spaced, by_row)

    mains = [c_body[8 + 8 * j : 16 + 8 * j, :] for j in range(TILES)]
    parts = [c_body[0:8, 32 * j : 32 * j + 32] for j in range(4)]
    parts += [c_rest[c // 4 : c // 4 + 1, 32 * (c % 4) : 32 * (c % 4) + 32] for c in range(8)]
    main = padded(jnp.concatenate(mains, axis=0), 128, 128).T
    tail = padded(jnp.concatenate(parts, axis=0), 128, 128).T
    crps_ref[0:16] = main[:, 0:per].reshape(16, COLS, per)
    crps_ref[16:20] = tail[0:32, 0:per].reshape(4, COLS, per)

    def tile_tail(d, j):
        return recv2[d, 0:8, 32 * j : 32 * j + 32] if j < 4 else tails[d, :, 0:32]

    def returned(step):
        peers(lambda other: body_copy(1, step, send2, recv2, other, other).wait_recv())
        if step == 0:
            peers(lambda other: rest_copy(1, rest2, got2, other, other).wait_recv())
            gather_rest(got2, tails)
        for j in STEPS[step]:
            mains, parts = [], []
            for d in range(n_ens):
                at = slice(8 * (TILES * d + j), 8 * (TILES * d + j) + 8)
                mains.append(recv2[d, 8 + 8 * j : 16 + 8 * j, :] * damp_main[at, :])
                parts.append(tile_tail(d, j) * damp_tail[at, 0:32])
            main = jnp.concatenate(mains, axis=0).T
            tail = padded(jnp.concatenate(parts, axis=0), 128, 128).T
            cols = slice(128 * j, 128 * j + 128)
            field[0:16, :, cols] = main.reshape(16, COLS, 128)
            field[16:20, :, cols] = tail[0:32].reshape(4, COLS, 128)
        cols = slice(128 * STEPS[step][0], 128 * STEPS[step][-1] + 128)
        fill_packs(field, cols)
        start_halo(3 + step, field, cols)

    def adjoint(step):
        inputs = slice(128 * STEPS[step][0], 128 * STEPS[step][-1] + 128)
        extend(3 + step, field, inputs)
        stencil(inputs)
        for cols in chunks():
            more = mix(cols, inputs).reshape(ROWS, COLS, cols.stop - cols.start)
            grad_ref[:, :, cols] = more if step == 0 else grad_ref[:, :, cols] + more

    for step in range(3):
        returned(step)
    adjoint(0)
    adjoint(1)
    for c in range(channels // 128):
        mains, parts = [], []
        for n in range(16):
            k = 16 * c + n
            d, j = k // TILES, k % TILES
            mains.append(recv2[d, 8 + 8 * j : 16 + 8 * j, :])
            parts.append(tile_tail(d, j))
        main = jnp.concatenate(mains, axis=0).T
        tail = padded(jnp.concatenate(parts, axis=0), 128, 128).T
        cols = slice(128 * c, 128 * c + 128)
        grad_ref[0:16, :, cols] = grad_ref[0:16, :, cols] + main.reshape(16, COLS, 128)
        grad_ref[16:20, :, cols] = grad_ref[16:20, :, cols] + tail[0:32].reshape(4, COLS, 128)
    adjoint(2)
    for step, cols in enumerate(chunks()):
        halo_sent(3 + step, field, cols)
    for phase, body, rest, there, got in ((0, send1, rest1, recv1, got1), (1, send2, rest2, recv2, got2)):
        for step in range(3):
            peers(lambda other: body_copy(phase, step, body, there, other, ens).wait_send())
        peers(lambda other: rest_copy(phase, rest, got, other, ens).wait_send())


def keep(grad_ref, crps_ref, grad_out, crps_out):
    grad_out[...] = grad_ref[...]
    crps_out[...] = crps_ref[...]


def local(members, analysis, stencils, mixing):
    channels = members.shape[3]
    n_ens = lax.axis_size("ens")
    per = channels // n_ens
    depth = BASES * channels
    cells = ROWS * COLS
    vmem = pl.BlockSpec(memory_space=pltpu.VMEM)
    body = pltpu.VMEM((n_ens, BODY, 128), f32)
    rest = pltpu.VMEM((n_ens, 2, 128), f32)
    grad, crps = pl.pallas_call(
        step_kernel,
        out_shape=[
            jax.ShapeDtypeStruct((ROWS, COLS, channels), f32),
            jax.ShapeDtypeStruct((ROWS, COLS, per), f32),
        ],
        in_specs=[pl.BlockSpec(memory_space=pl.ANY)] * 4,
        out_specs=[vmem, vmem],
        scratch_shapes=[
            pltpu.VMEM(members.shape[1:], f32),
            pltpu.VMEM(analysis.shape, f32),
            pltpu.VMEM(stencils.shape, f32),
            pltpu.SemaphoreType.DMA((3,)),
            pltpu.VMEM((WINDOWS, 16 * BASES, 128), bf16),
            pltpu.VMEM((WINDOWS, 16 * BASES, 128), bf16),
            pltpu.VMEM((128, 128), f32),
            pltpu.VMEM((128, 128), f32),
            pltpu.VMEM((BASES, channels, channels), f32),
            pltpu.VMEM((channels, channels), f32),
            pltpu.VMEM((depth, channels), bf16),
            pltpu.VMEM((depth, channels), bf16),
            pltpu.VMEM((16 * EXT, channels), bf16),
            pltpu.VMEM((16 * EXT, channels), bf16),
            pltpu.VMEM((cells, depth), bf16),
            pltpu.VMEM((cells, depth), bf16),
            pltpu.VMEM((ROWS, COLS, channels), f32),
            pltpu.VMEM((cells, channels), f32),
            pltpu.VMEM((channels, 128), f32),
            pltpu.VMEM((channels, 128), f32),
            pltpu.VMEM((64, channels), f32),
            pltpu.VMEM((64, channels), f32),
            pltpu.VMEM((2, 2, 64, channels), f32),
            pltpu.VMEM((2, 2, MARGIN, COLS, channels), f32),
            pltpu.VMEM((2, 4, 16, channels), f32),
            pltpu.VMEM((BODY, 128), f32),
            pltpu.VMEM((2, 128), f32),
            pltpu.VMEM((BODY, 128), f32),
            pltpu.VMEM((2, 128), f32),
            pltpu.VMEM((n_ens, 8, 128), f32),
            body, rest, body, rest,
            body, rest, body, rest,
            pltpu.SemaphoreType.DMA((3,)),
            pltpu.SemaphoreType.DMA((6, 8)),
            pltpu.SemaphoreType.DMA((6, 8)),
            pltpu.SemaphoreType.DMA((2, 4, n_ens)),
            pltpu.SemaphoreType.DMA((2, 4, n_ens)),
        ],
        compiler_params=pltpu.CompilerParams(
            collective_id=0, has_side_effects=True, vmem_limit_bytes=56 * 1024 * 1024
        ),
        name="ensemble_step",
    )(members[0], analysis, stencils, mixing)
    grad, crps = pl.pallas_call(
        keep,
        out_shape=[jax.ShapeDtypeStruct(grad.shape, f32), jax.ShapeDtypeStruct(crps.shape, f32)],
        in_specs=[vmem] * 2,
        out_specs=[vmem] * 2,
        name="results",
    )(grad, crps)
    return grad[None], crps


def solution(mesh):
    in_specs = (P("ens", "lat", "lon", None), P("lat", "lon", "ens"), P(), P())
    out_specs = (P("ens", "lat", "lon", None), P("lat", "lon", "ens"))
    return jax.shard_map(local, mesh=mesh, in_specs=in_specs, out_specs=out_specs, check_vma=False)
```

```python
import functools

import jax
import jax.numpy as jnp
import numpy as np
from jax import lax
from jax.experimental import pallas as pl
from jax.experimental.pallas import tpu as pltpu
from jax.sharding import PartitionSpec as P

BASES = 7
SPAN = 7
MARGIN = 3
ROWS = 20
COLS = 8
WINDOWS = ROWS // 2
EXT = ROWS + 2 * MARGIN
SMOOTH = 0.01
MESH = pl.DeviceIdType.MESH
f32 = jnp.float32
bf16 = jnp.bfloat16


def split(x):
    hi = x.astype(bf16)
    return hi, (x - hi.astype(f32)).astype(bf16)


def mm(a, b):
    return jnp.dot(a, b, preferred_element_type=f32)


def stencil_matrices(kind, st_ref, hi_ref, lo_ref, spaced, by_row):
    lat_rows = st_ref.shape[3]
    first = lax.axis_index("lat") * ROWS
    lane = lax.broadcasted_iota(jnp.int32, (8, 128), 1)
    wrapped = (lane % 16) >= 11
    spaced[...] = jnp.zeros_like(spaced)

    def one_basis(b, carry):
        for p in range(SPAN):
            if kind == 0:
                spaced[16 * p : 16 * p + SPAN, 0:lat_rows] = st_ref[b, p]
            else:
                for q in range(SPAN):
                    r = 16 * p + q
                    spaced[r : r + 1, 0:lat_rows] = st_ref[b, SPAN - 1 - p, SPAN - 1 - q : SPAN - q, :]
        if kind == 0:
            lines = spaced[...]
        else:
            lines = jnp.concatenate(
                [pltpu.roll(spaced[16 * p : 16 * p + 16, :], (MARGIN - p) % 128, 1) for p in range(8)], axis=0
            )
        by_row[...] = pltpu.roll(lines.T, 128 - MARGIN, 1)
        at = pl.ds(pl.multiple_of(16 * b, 16), 16)
        for u in range(WINDOWS):
            rows = []
            for i01 in range(2):
                line = jnp.broadcast_to(by_row[pl.ds(first + 2 * u + i01, 1), :], (8, 128))
                shifted = pltpu.roll(line, 16 * i01, 1, stride=1, stride_axis=0)
                rows.append(jnp.where(wrapped, pltpu.roll(shifted, 16, 1), shifted))
            hi_ref[u, at, :], lo_ref[u, at, :] = split(jnp.concatenate(rows, axis=0))
        return carry

    lax.fori_loop(0, BASES, one_basis, 0)


TILES = 5
LAST = 8 * (TILES + 1)
PIECE = LAST + 2
PARTS = ((0, 24), (24, PIECE - 24))
STEPS = ((0, 1), (2, 3), (4,))


def spread_rest(tails, pieces):
    for c in range(8):
        row = LAST + c // 4
        pieces[:, row, 32 * (c % 4) : 32 * (c % 4) + 32] = tails[:, c, 0:32]


def gather_rest(pieces, tails):
    for c in range(8):
        row = LAST + c // 4
        tails[:, c, 0:32] = pieces[:, row, 32 * (c % 4) : 32 * (c % 4) + 32]


def padded(x, rows, lanes):
    if x.shape[1] < lanes:
        x = jnp.concatenate([x, jnp.zeros((x.shape[0], lanes - x.shape[1]), f32)], axis=1)
    if x.shape[0] < rows:
        x = jnp.concatenate([x, jnp.zeros((rows - x.shape[0], lanes), f32)], axis=0)
    return x


def step_kernel(
    members_hbm, analysis_hbm, stencils_hbm, mixing_ref,
    grad_ref, crps_ref,
    members_ref, analysis_ref, stencils_ref, in_sem,
    w_hi, w_lo, spaced, by_row, staged, turned, m_hi, m_lo, e_hi, e_lo, s_hi, s_lo,
    field, act, damp_main, damp_tail, pack_r, pack_l, side, updown, corner,
    a_piece, c_piece, tails, send1, recv1, send2, recv2,
    mix_sem, halo_send, halo_recv, a2a_send, a2a_recv,
):
    n_ens = lax.axis_size("ens")
    n_lat = lax.axis_size("lat")
    n_lon = lax.axis_size("lon")
    ens, lat, lon = lax.axis_index("ens"), lax.axis_index("lat"), lax.axis_index("lon")
    right, left = lax.rem(lon + 1, n_lon), lax.rem(lon + n_lon - 1, n_lon)
    has_up, has_down = lat > 0, lat < n_lat - 1
    channels = members_hbm.shape[2]
    cells = ROWS * COLS
    per = 8 * TILES

    def chunks():
        return [slice(c, min(c + 256, channels)) for c in range(0, channels, 256)]

    loads = [
        pltpu.make_async_copy(src, dst, in_sem.at[k])
        for k, (src, dst) in enumerate(
            ((members_hbm, members_ref), (stencils_hbm, stencils_ref), (analysis_hbm, analysis_ref))
        )
    ]
    for load in loads:
        load.start()

    def weights_copy(n, cols):
        rows = pl.ds(cols.start, cols.stop - cols.start)
        return pltpu.make_async_copy(mixing_ref.at[:, rows], staged.at[:, rows], mix_sem.at[n])

    for n, cols in enumerate(chunks()):
        weights_copy(n, cols).start()

    barrier = pltpu.get_barrier_semaphore()

    def greet(k, carry):
        pl.semaphore_signal(barrier, 1, device_id={"ens": lax.rem(ens + k, n_ens)}, device_id_type=MESH)
        return carry

    lax.fori_loop(1, n_ens, greet, 0)
    for side_lon in (left, right):
        pl.semaphore_signal(barrier, 1, device_id={"lon": side_lon}, device_id_type=MESH)
    for there, other in ((has_up, lat - 1), (has_down, lat + 1)):
        @pl.when(there)
        def _():
            pl.semaphore_signal(barrier, 1, device_id={"lat": other}, device_id_type=MESH)
            for side_lon in (left, right):
                pl.semaphore_signal(barrier, 1, device_id={"lat": other, "lon": side_lon}, device_id_type=MESH)

    def fill_packs(src, cols):
        for r in range(ROWS):
            pack_r[3 * r : 3 * r + 3, cols] = src[r, COLS - MARGIN : COLS, cols]
            pack_l[3 * r : 3 * r + 3, cols] = src[r, 0:MARGIN, cols]

    every = slice(0, channels)
    pack_r[56:64, :] = jnp.zeros((8, channels), f32)
    pack_l[56:64, :] = jnp.zeros((8, channels), f32)
    for load in loads:
        load.wait()
    fill_packs(members_ref, every)
    pl.semaphore_wait(barrier, n_ens + 1 + 3 * has_up.astype(jnp.int32) + 3 * has_down.astype(jnp.int32))

    def halo_copies(phase, src, cols):
        back = phase // 3
        lanes = pl.ds(cols.start, cols.stop - cols.start)

        def remote(k, a, b, to):
            return pltpu.make_async_remote_copy(
                a, b, halo_send.at[phase, k], halo_recv.at[phase, k], device_id=to, device_id_type=MESH
            )

        up, down = lat - 1, lat + 1
        low = pl.ds(0, 16)
        high = pl.ds(48, 16)
        return [
            (None, None, remote(0, pack_r.at[:, lanes], side.at[back, 0, :, lanes], {"lon": right})),
            (None, None, remote(1, pack_l.at[:, lanes], side.at[back, 1, :, lanes], {"lon": left})),
            (
                has_down, has_up,
                remote(2, src.at[pl.ds(ROWS - 3, 3), :, lanes], updown.at[back, 0, :, :, lanes], {"lat": down}),
            ),
            (
                has_up, has_down,
                remote(3, src.at[pl.ds(0, 3), :, lanes], updown.at[back, 1, :, :, lanes], {"lat": up}),
            ),
            (
                has_down, has_up,
                remote(4, pack_r.at[high, lanes], corner.at[back, 0, :, lanes], {"lat": down, "lon": right}),
            ),
            (
                has_down, has_up,
                remote(5, pack_l.at[high, lanes], corner.at[back, 1, :, lanes], {"lat": down, "lon": left}),
            ),
            (
                has_up, has_down,
                remote(6, pack_r.at[low, lanes], corner.at[back, 2, :, lanes], {"lat": up, "lon": right}),
            ),
            (
                has_up, has_down,
                remote(7, pack_l.at[low, lanes], corner.at[back, 3, :, lanes], {"lat": up, "lon": left}),
            ),
        ]

    def start_halo(phase, src, cols):
        for sends, _, copy in halo_copies(phase, src, cols):
            if sends is None:
                copy.start()
            else:
                pl.when(sends)(copy.start)

    def put_row(r, inner, from_right, from_left, cols):
        gap = jnp.zeros((2, cols.stop - cols.start), f32)
        hi, lo = split(jnp.concatenate([inner, from_right, gap, from_left], axis=0))
        e_hi[16 * r : 16 * r + 16, cols] = hi
        e_lo[16 * r : 16 * r + 16, cols] = lo

    def extend(phase, src, cols):
        copies = halo_copies(phase, src, cols)
        back = phase // 3
        for k in (0, 1):
            copies[k][2].wait_recv()
        for r in range(ROWS):
            at = slice(3 * r, 3 * r + 3)
            put_row(r + MARGIN, src[r, :, cols], side[back, 1, at, cols], side[back, 0, at, cols], cols)
        for there, which, corners, first, offset in (
            (has_up, 0, (0, 1), 0, 3),
            (has_down, 1, (2, 3), ROWS + MARGIN, 0),
        ):
            @pl.when(there)
            def _():
                for k in (2 + which, 4 + 2 * which, 5 + 2 * which):
                    copies[k][2].wait_recv()
                for r in range(3):
                    at = slice(offset + 3 * r, offset + 3 * r + 3)
                    put_row(
                        first + r, updown[back, which, r, :, cols],
                        corner[back, corners[1], at, cols], corner[back, corners[0], at, cols], cols,
                    )

            @pl.when(jnp.logical_not(there))
            def _():
                for ref in (e_hi, e_lo):
                    ref[16 * first : 16 * first + 48, cols] = jnp.zeros((48, cols.stop - cols.start), bf16)

    def halo_sent(phase, src, cols):
        for sends, _, copy in halo_copies(phase, src, cols):
            if sends is None:
                copy.wait_send()
            else:
                pl.when(sends)(copy.wait_send)

    def stencil(cols):
        width = cols.stop - cols.start

        def one_window(u, carry):
            at = pl.ds(pl.multiple_of(32 * u, 32), 128)
            x_hi, x_lo = e_hi[at, cols], e_lo[at, cols]
            wh = w_hi[u]
            out = mm(jnp.concatenate([wh, wh], axis=1), jnp.concatenate([x_hi, x_lo], axis=0)) + mm(w_lo[u], x_hi)
            hi, lo = split(out)
            to = pl.ds(pl.multiple_of(16 * u, 16), 16)
            for b in range(BASES):
                here = slice(BASES * cols.start + b * width, BASES * cols.start + (b + 1) * width)
                s_hi[to, here] = hi[16 * b : 16 * b + 16]
                s_lo[to, here] = lo[16 * b : 16 * b + 16]
            return carry

        lax.fori_loop(0, WINDOWS, one_window, 0, unroll=True)

    def mix(cols, inputs):
        k = slice(BASES * inputs.start, BASES * inputs.stop)
        weights, more = m_hi[k, cols], m_lo[k, cols]
        width = cols.stop - cols.start
        if width == 128:
            both = mm(s_hi[:, k], jnp.concatenate([weights, more], axis=1))
            return both[:, :128] + both[:, 128:] + mm(s_lo[:, k], weights)
        return mm(s_hi[:, k], weights) + mm(s_lo[:, k], weights) + mm(s_hi[:, k], more)

    def load_weights(n, cols):
        weights_copy(n, cols).wait()
        width = cols.stop - cols.start

        def one_basis(b, carry):
            for k in range(width // 128):
                at = cols.start + 128 * k
                hi, lo = split(staged[b, at : at + 128, :])
                to = pl.ds(pl.multiple_of(BASES * cols.start + b * width + 128 * k, 128), 128)
                m_hi[to, :] = hi
                m_lo[to, :] = lo
            return carry

        lax.fori_loop(0, BASES, one_basis, 0)

    def transpose_weights(b, carry):
        for k in range(channels // 128):
            turned[128 * k : 128 * k + 128, :] = staged[b, :, 128 * k : 128 * k + 128].T
        for first, tiles in ((128 * step[0], step) for step in STEPS):
            width = 128 * len(tiles)
            for n, j in enumerate(tiles):
                for d in range(0, n_ens, 2):
                    low, high = 8 * (TILES * d + j), 8 * (TILES * (d + 1) + j)
                    hi, lo = split(jnp.concatenate([turned[low : low + 8, :], turned[high : high + 8, :]], axis=0))
                    to = pl.ds(pl.multiple_of(BASES * first + b * width + 128 * n + 8 * d, 16), 16)
                    m_hi[to, :] = hi
                    m_lo[to, :] = lo
        return carry

    for n, cols in enumerate(chunks()):
        start_halo(n, members_ref, cols)
    stencil_matrices(0, stencils_ref, w_hi, w_lo, spaced, by_row)

    for n, inputs in enumerate(chunks()):
        load_weights(n, inputs)
        extend(n, members_ref, inputs)
        stencil(inputs)

    def exchange(phase, part, src, dst, other, slot):
        first, count = PARTS[part]
        rows = pl.ds(first, count)
        return pltpu.make_async_remote_copy(
            src.at[other, rows], dst.at[slot, rows], a2a_send.at[phase, part, other], a2a_recv.at[phase, part, slot],
            device_id={"ens": other}, device_id_type=MESH,
        )

    def peers(action):
        def one(k, carry):
            action(lax.rem(ens + k, n_ens))
            return carry

        lax.fori_loop(1, n_ens, one, 0)

    for cols in chunks():
        width = cols.stop - cols.start
        activation = jnp.tanh(mix(cols, every))
        act[:, cols] = activation
        forecast = members_ref[:, :, cols].reshape(cells, width) + activation
        for c in range(width // 128):
            part = forecast[:, 128 * c : 128 * c + 128]
            main, tail = part[:128].T, padded(part[128:], 128, 128).T
            for n in range(16):
                k = (cols.start // 128 + c) * 16 + n
                d, j = k // TILES, k % TILES
                send1[d, 8 + 8 * j : 16 + 8 * j, :] = main[8 * n : 8 * n + 8]
                if j < 4:
                    send1[d, 0:8, 32 * j : 32 * j + 32] = tail[8 * n : 8 * n + 8, 0:32]
                else:
                    tails[d, :, 0:32] = tail[8 * n : 8 * n + 8, 0:32]
    peers(lambda other: exchange(0, 0, send1, recv1, other, ens).start())
    spread_rest(tails, send1)
    peers(lambda other: exchange(0, 1, send1, recv1, other, ens).start())
    recv1[ens] = send1[ens]

    for n, cols in enumerate(chunks()):
        halo_sent(n, members_ref, cols)

    truth = padded(analysis_ref[...].reshape(cells, per), cells, 128)
    main, tail = truth[:128].T, padded(truth[128:], 128, 128).T
    for j in range(TILES):
        a_piece[8 + 8 * j : 16 + 8 * j, :] = main[8 * j : 8 * j + 8]
        if j < 4:
            a_piece[0:8, 32 * j : 32 * j + 32] = tail[8 * j : 8 * j + 8, 0:32]
        else:
            for c in range(8):
                row = LAST + c // 4
                a_piece[row : row + 1, 32 * (c % 4) : 32 * (c % 4) + 32] = tail[8 * j + c : 8 * j + c + 1, 0:32]

    lax.fori_loop(0, BASES, transpose_weights, 0)
    for c in range(channels // 128):
        damp = act[:, 128 * c : 128 * c + 128]
        damp = 1.0 - damp * damp
        damp_main[128 * c : 128 * c + 128, :] = damp[:128].T
        damp_tail[128 * c : 128 * c + 128, :] = padded(damp[128:], 128, 128).T

    members_total = n_ens
    diagonal = members_total * float(np.sqrt(np.float32(SMOOTH)))
    pairs_scale = 2.0 * members_total * (members_total - 1)

    def score(read, truth, write):
        x = [read(m) - truth for m in range(n_ens)]
        slope = [None] * n_ens
        own, pair_abs = None, None
        for m in range(n_ens):
            for n in range(m + 1, n_ens):
                d = x[m] - x[n]
                s2 = d * d + SMOOTH
                r = lax.rsqrt(s2)
                sl = d * r
                ab = s2 * r
                pair_abs = ab if pair_abs is None else pair_abs + ab
                slope[m] = sl if slope[m] is None else slope[m] + sl
                slope[n] = -sl if slope[n] is None else slope[n] - sl
            s2 = x[m] * x[m] + SMOOTH
            r = lax.rsqrt(s2)
            own = s2 * r if own is None else own + s2 * r
            write(m, x[m] * r - slope[m] * (1.0 / (members_total - 1.0)))
        return own * (1.0 / members_total) - (2.0 * pair_abs + diagonal) * (1.0 / pairs_scale)

    def score_rows(t, carry):
        rows = pl.ds(pl.multiple_of(8 * t, 8), 8)

        def write(m, value):
            send2[m, rows, :] = value

        c_piece[rows, :] = score(lambda m: recv1[m, rows, :], a_piece[rows, :], write)
        return carry

    for part in range(2):
        peers(lambda other: exchange(0, part, send1, recv1, other, other).wait_recv())
        first, count = PARTS[part]
        lax.fori_loop(first // 8, (first + count) // 8, score_rows, 0)
        if part == 1:
            rows = slice(LAST, PIECE)

            def write_last(m, value):
                send2[m, rows, :] = value

            c_piece[rows, :] = score(lambda m: recv1[m, rows, :], a_piece[rows, :], write_last)
        peers(lambda other: exchange(1, part, send2, recv2, other, ens).start())
    recv2[ens] = send2[ens]
    stencil_matrices(1, stencils_ref, w_hi, w_lo, spaced, by_row)

    mains = [c_piece[8 + 8 * j : 16 + 8 * j, :] for j in range(TILES)]
    parts = [c_piece[0:8, 32 * j : 32 * j + 32] for j in range(4)]
    for c in range(8):
        row = LAST + c // 4
        parts.append(c_piece[row : row + 1, 32 * (c % 4) : 32 * (c % 4) + 32])
    main = padded(jnp.concatenate(mains, axis=0), 128, 128).T
    tail = padded(jnp.concatenate(parts, axis=0), 128, 128).T
    crps_ref[0:16] = main[:, 0:per].reshape(16, COLS, per)
    crps_ref[16:20] = tail[0:32, 0:per].reshape(4, COLS, per)

    def tile_tail(d, j):
        return recv2[d, 0:8, 32 * j : 32 * j + 32] if j < 4 else tails[d, :, 0:32]

    def returned(step):
        if step < 2:
            peers(lambda other: exchange(1, step, send2, recv2, other, other).wait_recv())
        if step == 1:
            gather_rest(recv2, tails)
        for j in STEPS[step]:
            mains, parts = [], []
            for d in range(n_ens):
                at = slice(8 * (TILES * d + j), 8 * (TILES * d + j) + 8)
                mains.append(recv2[d, 8 + 8 * j : 16 + 8 * j, :] * damp_main[at, :])
                parts.append(tile_tail(d, j) * damp_tail[at, 0:32])
            main = jnp.concatenate(mains, axis=0).T
            tail = padded(jnp.concatenate(parts, axis=0), 128, 128).T
            cols = slice(128 * j, 128 * j + 128)
            field[0:16, :, cols] = main.reshape(16, COLS, 128)
            field[16:20, :, cols] = tail[0:32].reshape(4, COLS, 128)
        cols = slice(128 * STEPS[step][0], 128 * STEPS[step][-1] + 128)
        fill_packs(field, cols)
        start_halo(3 + step, field, cols)

    def adjoint(step):
        inputs = slice(128 * STEPS[step][0], 128 * STEPS[step][-1] + 128)
        extend(3 + step, field, inputs)
        stencil(inputs)
        for cols in chunks():
            more = mix(cols, inputs).reshape(ROWS, COLS, cols.stop - cols.start)
            grad_ref[:, :, cols] = more if step == 0 else grad_ref[:, :, cols] + more

    for step in range(3):
        returned(step)
    adjoint(0)
    adjoint(1)
    for c in range(channels // 128):
        mains, parts = [], []
        for n in range(16):
            k = 16 * c + n
            d, j = k // TILES, k % TILES
            mains.append(recv2[d, 8 + 8 * j : 16 + 8 * j, :])
            parts.append(tile_tail(d, j))
        main = jnp.concatenate(mains, axis=0).T
        tail = padded(jnp.concatenate(parts, axis=0), 128, 128).T
        cols = slice(128 * c, 128 * c + 128)
        grad_ref[0:16, :, cols] = grad_ref[0:16, :, cols] + main.reshape(16, COLS, 128)
        grad_ref[16:20, :, cols] = grad_ref[16:20, :, cols] + tail[0:32].reshape(4, COLS, 128)
    adjoint(2)
    for step, cols in enumerate(chunks()):
        halo_sent(3 + step, field, cols)
    for phase, src, dst in ((0, send1, recv1), (1, send2, recv2)):
        for part in range(2):
            peers(lambda other: exchange(phase, part, src, dst, other, ens).wait_send())


def keep(grad_ref, crps_ref, grad_out, crps_out):
    grad_out[...] = grad_ref[...]
    crps_out[...] = crps_ref[...]


def local(members, analysis, stencils, mixing):
    channels = members.shape[3]
    n_ens = lax.axis_size("ens")
    per = channels // n_ens
    depth = BASES * channels
    cells = ROWS * COLS
    vmem = pl.BlockSpec(memory_space=pltpu.VMEM)
    pieces = pltpu.VMEM((n_ens, PIECE, 128), f32)
    grad, crps = pl.pallas_call(
        step_kernel,
        out_shape=[
            jax.ShapeDtypeStruct((ROWS, COLS, channels), f32),
            jax.ShapeDtypeStruct((ROWS, COLS, per), f32),
        ],
        in_specs=[pl.BlockSpec(memory_space=pl.ANY)] * 4,
        out_specs=[vmem, vmem],
        scratch_shapes=[
            pltpu.VMEM(members.shape[1:], f32),
            pltpu.VMEM(analysis.shape, f32),
            pltpu.VMEM(stencils.shape, f32),
            pltpu.SemaphoreType.DMA((3,)),
            pltpu.VMEM((WINDOWS, 16 * BASES, 128), bf16),
            pltpu.VMEM((WINDOWS, 16 * BASES, 128), bf16),
            pltpu.VMEM((128, 128), f32),
            pltpu.VMEM((128, 128), f32),
            pltpu.VMEM((BASES, channels, channels), f32),
            pltpu.VMEM((channels, channels), f32),
            pltpu.VMEM((depth, channels), bf16),
            pltpu.VMEM((depth, channels), bf16),
            pltpu.VMEM((16 * EXT, channels), bf16),
            pltpu.VMEM((16 * EXT, channels), bf16),
            pltpu.VMEM((cells, depth), bf16),
            pltpu.VMEM((cells, depth), bf16),
            pltpu.VMEM((ROWS, COLS, channels), f32),
            pltpu.VMEM((cells, channels), f32),
            pltpu.VMEM((channels, 128), f32),
            pltpu.VMEM((channels, 128), f32),
            pltpu.VMEM((64, channels), f32),
            pltpu.VMEM((64, channels), f32),
            pltpu.VMEM((2, 2, 64, channels), f32),
            pltpu.VMEM((2, 2, MARGIN, COLS, channels), f32),
            pltpu.VMEM((2, 4, 16, channels), f32),
            pltpu.VMEM((PIECE, 128), f32),
            pltpu.VMEM((PIECE, 128), f32),
            pltpu.VMEM((n_ens, 8, 128), f32),
            pieces, pieces, pieces, pieces,
            pltpu.SemaphoreType.DMA((3,)),
            pltpu.SemaphoreType.DMA((6, 8)),
            pltpu.SemaphoreType.DMA((6, 8)),
            pltpu.SemaphoreType.DMA((2, 2, n_ens)),
            pltpu.SemaphoreType.DMA((2, 2, n_ens)),
        ],
        compiler_params=pltpu.CompilerParams(
            collective_id=0, has_side_effects=True, vmem_limit_bytes=56 * 1024 * 1024
        ),
        name="ensemble_step",
    )(members[0], analysis, stencils, mixing)
    grad, crps = pl.pallas_call(
        keep,
        out_shape=[jax.ShapeDtypeStruct(grad.shape, f32), jax.ShapeDtypeStruct(crps.shape, f32)],
        in_specs=[vmem] * 2,
        out_specs=[vmem] * 2,
        name="results",
    )(grad, crps)
    return grad[None], crps


def solution(mesh):
    in_specs = (P("ens", "lat", "lon", None), P("lat", "lon", "ens"), P(), P())
    out_specs = (P("ens", "lat", "lon", None), P("lat", "lon", "ens"))
    return jax.shard_map(local, mesh=mesh, in_specs=in_specs, out_specs=out_specs, check_vma=False)
```

```python
import functools

import jax
import jax.numpy as jnp
import numpy as np
from jax import lax
from jax.experimental import pallas as pl
from jax.experimental.pallas import tpu as pltpu
from jax.sharding import PartitionSpec as P

BASES = 7
SPAN = 7
MARGIN = 3
ROWS = 20
COLS = 8
WINDOWS = ROWS // 2
EXT = ROWS + 2 * MARGIN
SMOOTH = 0.01
MESH = pl.DeviceIdType.MESH
f32 = jnp.float32
bf16 = jnp.bfloat16


def split(x):
    hi = x.astype(bf16)
    return hi, (x - hi.astype(f32)).astype(bf16)


def mm(a, b):
    return jnp.dot(a, b, preferred_element_type=f32)


def stencil_matrices(kind, st_ref, hi_ref, lo_ref, spaced, by_row):
    lat_rows = st_ref.shape[3]
    first = lax.axis_index("lat") * ROWS
    lane = lax.broadcasted_iota(jnp.int32, (8, 128), 1)
    wrapped = (lane % 16) >= 11
    spaced[...] = jnp.zeros_like(spaced)

    def one_basis(b, carry):
        for p in range(SPAN):
            if kind == 0:
                spaced[16 * p : 16 * p + SPAN, 0:lat_rows] = st_ref[b, p]
            else:
                for q in range(SPAN):
                    r = 16 * p + q
                    spaced[r : r + 1, 0:lat_rows] = st_ref[b, SPAN - 1 - p, SPAN - 1 - q : SPAN - q, :]
        if kind == 0:
            lines = spaced[...]
        else:
            lines = jnp.concatenate(
                [pltpu.roll(spaced[16 * p : 16 * p + 16, :], (MARGIN - p) % 128, 1) for p in range(8)], axis=0
            )
        by_row[...] = pltpu.roll(lines.T, 128 - MARGIN, 1)
        at = pl.ds(pl.multiple_of(16 * b, 16), 16)
        for u in range(WINDOWS):
            rows = []
            for i01 in range(2):
                line = jnp.broadcast_to(by_row[pl.ds(first + 2 * u + i01, 1), :], (8, 128))
                shifted = pltpu.roll(line, 16 * i01, 1, stride=1, stride_axis=0)
                rows.append(jnp.where(wrapped, pltpu.roll(shifted, 16, 1), shifted))
            hi_ref[u, at, :], lo_ref[u, at, :] = split(jnp.concatenate(rows, axis=0))
        return carry

    lax.fori_loop(0, BASES, one_basis, 0)


TILES = 5
LAST = 8 * (TILES + 1)
PIECE = LAST + 2
PARTS = ((0, 24), (24, PIECE - 24))
STEPS = ((0, 1), (2, 3), (4,))


def spread_rest(tails, pieces):
    for c in range(8):
        row = LAST + c // 4
        pieces[:, row, 32 * (c % 4) : 32 * (c % 4) + 32] = tails[:, c, 0:32]


def gather_rest(pieces, tails):
    for c in range(8):
        row = LAST + c // 4
        tails[:, c, 0:32] = pieces[:, row, 32 * (c % 4) : 32 * (c % 4) + 32]


def padded(x, rows, lanes):
    if x.shape[1] < lanes:
        x = jnp.concatenate([x, jnp.zeros((x.shape[0], lanes - x.shape[1]), f32)], axis=1)
    if x.shape[0] < rows:
        x = jnp.concatenate([x, jnp.zeros((rows - x.shape[0], lanes), f32)], axis=0)
    return x


def step_kernel(
    members_hbm, analysis_hbm, stencils_hbm, mixing_ref,
    grad_ref, crps_ref,
    members_ref, analysis_ref, stencils_ref, in_sem,
    w_hi, w_lo, spaced, by_row, staged, turned, m_hi, m_lo, e_hi, e_lo, s_hi, s_lo,
    field, act, damp_main, damp_tail, pack_r, pack_l, low_r, low_l, side, updown, above, below,
    a_piece, c_piece, tails, send1, recv1, send2, recv2,
    mix_sem, halo_send, halo_recv, a2a_send, a2a_recv,
):
    n_ens = lax.axis_size("ens")
    n_lat = lax.axis_size("lat")
    n_lon = lax.axis_size("lon")
    ens, lat, lon = lax.axis_index("ens"), lax.axis_index("lat"), lax.axis_index("lon")
    right, left = lax.rem(lon + 1, n_lon), lax.rem(lon + n_lon - 1, n_lon)
    has_up, has_down = lat > 0, lat < n_lat - 1
    channels = members_hbm.shape[2]
    cells = ROWS * COLS
    per = 8 * TILES

    def chunks():
        return [slice(c, min(c + 256, channels)) for c in range(0, channels, 256)]

    loads = [
        pltpu.make_async_copy(src, dst, in_sem.at[k])
        for k, (src, dst) in enumerate(
            ((members_hbm, members_ref), (stencils_hbm, stencils_ref), (analysis_hbm, analysis_ref))
        )
    ]
    for load in loads:
        load.start()

    def weights_copy(n, cols):
        rows = pl.ds(cols.start, cols.stop - cols.start)
        return pltpu.make_async_copy(mixing_ref.at[:, rows], staged.at[:, rows], mix_sem.at[n])

    for n, cols in enumerate(chunks()):
        weights_copy(n, cols).start()

    barrier = pltpu.get_barrier_semaphore()

    def greet(k, carry):
        pl.semaphore_signal(barrier, 1, device_id={"ens": lax.rem(ens + k, n_ens)}, device_id_type=MESH)
        return carry

    lax.fori_loop(1, n_ens, greet, 0)
    for side_lon in (left, right):
        pl.semaphore_signal(barrier, 1, device_id={"lon": side_lon}, device_id_type=MESH)
    for there, other in ((has_up, lat - 1), (has_down, lat + 1)):
        @pl.when(there)
        def _():
            pl.semaphore_signal(barrier, 1, device_id={"lat": other}, device_id_type=MESH)
            for side_lon in (left, right):
                pl.semaphore_signal(barrier, 1, device_id={"lat": other, "lon": side_lon}, device_id_type=MESH)

    def fill_packs(src, cols):
        for r in range(ROWS):
            pack_r[3 * r : 3 * r + 3, cols] = src[r, COLS - MARGIN : COLS, cols]
            pack_l[3 * r : 3 * r + 3, cols] = src[r, 0:MARGIN, cols]
            if r < MARGIN:
                low_r[3 * r : 3 * r + 3, cols] = src[r, COLS - MARGIN : COLS, cols]
                low_l[3 * r : 3 * r + 3, cols] = src[r, 0:MARGIN, cols]

    every = slice(0, channels)
    for load in loads:
        load.wait()
    fill_packs(members_ref, every)
    pl.semaphore_wait(barrier, n_ens + 1 + 3 * has_up.astype(jnp.int32) + 3 * has_down.astype(jnp.int32))

    def halo_copies(phase, src, cols):
        back = phase // 3
        lanes = pl.ds(cols.start, cols.stop - cols.start)

        def remote(k, a, b, to):
            return pltpu.make_async_remote_copy(
                a, b, halo_send.at[phase, k], halo_recv.at[phase, k], device_id=to, device_id_type=MESH
            )

        up, down = lat - 1, lat + 1
        high = pl.ds(48, 12)
        return [
            (None, None, remote(0, pack_r.at[:, lanes], side.at[back, 0, :, lanes], {"lon": right})),
            (None, None, remote(1, pack_l.at[:, lanes], side.at[back, 1, :, lanes], {"lon": left})),
            (
                has_down, has_up,
                remote(2, src.at[pl.ds(ROWS - 3, 3), :, lanes], updown.at[back, 0, :, :, lanes], {"lat": down}),
            ),
            (
                has_up, has_down,
                remote(3, src.at[pl.ds(0, 3), :, lanes], updown.at[back, 1, :, :, lanes], {"lat": up}),
            ),
            (
                has_down, has_up,
                remote(4, pack_r.at[high, lanes], above.at[back, 0, :, lanes], {"lat": down, "lon": right}),
            ),
            (
                has_down, has_up,
                remote(5, pack_l.at[high, lanes], above.at[back, 1, :, lanes], {"lat": down, "lon": left}),
            ),
            (
                has_up, has_down,
                remote(6, low_r.at[:, lanes], below.at[back, 0, :, lanes], {"lat": up, "lon": right}),
            ),
            (
                has_up, has_down,
                remote(7, low_l.at[:, lanes], below.at[back, 1, :, lanes], {"lat": up, "lon": left}),
            ),
        ]

    def start_halo(phase, src, cols):
        for sends, _, copy in halo_copies(phase, src, cols):
            if sends is None:
                copy.start()
            else:
                pl.when(sends)(copy.start)

    def put_row(r, inner, from_right, from_left, cols):
        gap = jnp.zeros((2, cols.stop - cols.start), f32)
        hi, lo = split(jnp.concatenate([inner, from_right, gap, from_left], axis=0))
        e_hi[16 * r : 16 * r + 16, cols] = hi
        e_lo[16 * r : 16 * r + 16, cols] = lo

    def extend(phase, src, cols):
        copies = halo_copies(phase, src, cols)
        back = phase // 3
        for k in (0, 1):
            copies[k][2].wait_recv()
        for r in range(ROWS):
            at = slice(3 * r, 3 * r + 3)
            put_row(r + MARGIN, src[r, :, cols], side[back, 1, at, cols], side[back, 0, at, cols], cols)
        for there, which, corner, first, offset in (
            (has_up, 0, above, 0, 3),
            (has_down, 1, below, ROWS + MARGIN, 0),
        ):
            @pl.when(there)
            def _():
                for k in (2 + which, 4 + 2 * which, 5 + 2 * which):
                    copies[k][2].wait_recv()
                for r in range(3):
                    at = slice(offset + 3 * r, offset + 3 * r + 3)
                    put_row(
                        first + r, updown[back, which, r, :, cols],
                        corner[back, 1, at, cols], corner[back, 0, at, cols], cols,
                    )

            @pl.when(jnp.logical_not(there))
            def _():
                for ref in (e_hi, e_lo):
                    ref[16 * first : 16 * first + 48, cols] = jnp.zeros((48, cols.stop - cols.start), bf16)

    def halo_sent(phase, src, cols):
        for sends, _, copy in halo_copies(phase, src, cols):
            if sends is None:
                copy.wait_send()
            else:
                pl.when(sends)(copy.wait_send)

    def stencil(cols):
        width = cols.stop - cols.start

        def one_window(u, carry):
            at = pl.ds(pl.multiple_of(32 * u, 32), 128)
            x_hi, x_lo = e_hi[at, cols], e_lo[at, cols]
            wh = w_hi[u]
            out = mm(jnp.concatenate([wh, wh], axis=1), jnp.concatenate([x_hi, x_lo], axis=0)) + mm(w_lo[u], x_hi)
            hi, lo = split(out)
            to = pl.ds(pl.multiple_of(16 * u, 16), 16)
            for b in range(BASES):
                here = slice(BASES * cols.start + b * width, BASES * cols.start + (b + 1) * width)
                s_hi[to, here] = hi[16 * b : 16 * b + 16]
                s_lo[to, here] = lo[16 * b : 16 * b + 16]
            return carry

        lax.fori_loop(0, WINDOWS, one_window, 0, unroll=True)

    def mix(cols, inputs):
        k = slice(BASES * inputs.start, BASES * inputs.stop)
        weights, more = m_hi[k, cols], m_lo[k, cols]
        width = cols.stop - cols.start
        if width == 128:
            both = mm(s_hi[:, k], jnp.concatenate([weights, more], axis=1))
            return both[:, :128] + both[:, 128:] + mm(s_lo[:, k], weights)
        return mm(s_hi[:, k], weights) + mm(s_lo[:, k], weights) + mm(s_hi[:, k], more)

    def load_weights(n, cols):
        weights_copy(n, cols).wait()
        width = cols.stop - cols.start

        def one_basis(b, carry):
            for k in range(width // 128):
                at = cols.start + 128 * k
                hi, lo = split(staged[b, at : at + 128, :])
                to = pl.ds(pl.multiple_of(BASES * cols.start + b * width + 128 * k, 128), 128)
                m_hi[to, :] = hi
                m_lo[to, :] = lo
            return carry

        lax.fori_loop(0, BASES, one_basis, 0)

    def transpose_weights(b, carry):
        for k in range(channels // 128):
            turned[128 * k : 128 * k + 128, :] = staged[b, :, 128 * k : 128 * k + 128].T
        for first, tiles in ((128 * step[0], step) for step in STEPS):
            width = 128 * len(tiles)
            for n, j in enumerate(tiles):
                for d in range(0, n_ens, 2):
                    low, high = 8 * (TILES * d + j), 8 * (TILES * (d + 1) + j)
                    hi, lo = split(jnp.concatenate([turned[low : low + 8, :], turned[high : high + 8, :]], axis=0))
                    to = pl.ds(pl.multiple_of(BASES * first + b * width + 128 * n + 8 * d, 16), 16)
                    m_hi[to, :] = hi
                    m_lo[to, :] = lo
        return carry

    for n, cols in enumerate(chunks()):
        start_halo(n, members_ref, cols)
    stencil_matrices(0, stencils_ref, w_hi, w_lo, spaced, by_row)

    for n, inputs in enumerate(chunks()):
        load_weights(n, inputs)
        extend(n, members_ref, inputs)
        stencil(inputs)

    def exchange(phase, part, src, dst, other, slot):
        first, count = PARTS[part]
        rows = pl.ds(first, count)
        return pltpu.make_async_remote_copy(
            src.at[other, rows], dst.at[slot, rows], a2a_send.at[phase, part, other], a2a_recv.at[phase, part, slot],
            device_id={"ens": other}, device_id_type=MESH,
        )

    def peers(action):
        def one(k, carry):
            action(lax.rem(ens + k, n_ens))
            return carry

        lax.fori_loop(1, n_ens, one, 0, unroll=True)

    for cols in chunks():
        width = cols.stop - cols.start
        activation = jnp.tanh(mix(cols, every))
        act[:, cols] = activation
        forecast = members_ref[:, :, cols].reshape(cells, width) + activation
        for c in range(width // 128):
            part = forecast[:, 128 * c : 128 * c + 128]
            main, tail = part[:128].T, padded(part[128:], 128, 128).T
            for n in range(16):
                k = (cols.start // 128 + c) * 16 + n
                d, j = k // TILES, k % TILES
                send1[d, 8 + 8 * j : 16 + 8 * j, :] = main[8 * n : 8 * n + 8]
                if j < 4:
                    send1[d, 0:8, 32 * j : 32 * j + 32] = tail[8 * n : 8 * n + 8, 0:32]
                else:
                    tails[d, :, 0:32] = tail[8 * n : 8 * n + 8, 0:32]
    peers(lambda other: exchange(0, 0, send1, recv1, other, ens).start())
    spread_rest(tails, send1)
    peers(lambda other: exchange(0, 1, send1, recv1, other, ens).start())
    recv1[ens] = send1[ens]

    for n, cols in enumerate(chunks()):
        halo_sent(n, members_ref, cols)

    truth = padded(analysis_ref[...].reshape(cells, per), cells, 128)
    main, tail = truth[:128].T, padded(truth[128:], 128, 128).T
    for j in range(TILES):
        a_piece[8 + 8 * j : 16 + 8 * j, :] = main[8 * j : 8 * j + 8]
        if j < 4:
            a_piece[0:8, 32 * j : 32 * j + 32] = tail[8 * j : 8 * j + 8, 0:32]
        else:
            for c in range(8):
                row = LAST + c // 4
                a_piece[row : row + 1, 32 * (c % 4) : 32 * (c % 4) + 32] = tail[8 * j + c : 8 * j + c + 1, 0:32]

    lax.fori_loop(0, BASES, transpose_weights, 0)
    for c in range(channels // 128):
        damp = act[:, 128 * c : 128 * c + 128]
        damp = 1.0 - damp * damp
        damp_main[128 * c : 128 * c + 128, :] = damp[:128].T
        damp_tail[128 * c : 128 * c + 128, :] = padded(damp[128:], 128, 128).T

    members_total = n_ens
    diagonal = members_total * float(np.sqrt(np.float32(SMOOTH)))
    pairs_scale = 2.0 * members_total * (members_total - 1)

    def score(read, truth, write):
        x = [read(m) - truth for m in range(n_ens)]
        slope = [None] * n_ens
        own, pair_abs = None, None
        for m in range(n_ens):
            for n in range(m + 1, n_ens):
                d = x[m] - x[n]
                s2 = d * d + SMOOTH
                r = lax.rsqrt(s2)
                sl = d * r
                ab = s2 * r
                pair_abs = ab if pair_abs is None else pair_abs + ab
                slope[m] = sl if slope[m] is None else slope[m] + sl
                slope[n] = -sl if slope[n] is None else slope[n] - sl
            s2 = x[m] * x[m] + SMOOTH
            r = lax.rsqrt(s2)
            own = s2 * r if own is None else own + s2 * r
            write(m, x[m] * r - slope[m] * (1.0 / (members_total - 1.0)))
        return own * (1.0 / members_total) - (2.0 * pair_abs + diagonal) * (1.0 / pairs_scale)

    def score_rows(t, carry):
        rows = pl.ds(pl.multiple_of(8 * t, 8), 8)

        def write(m, value):
            send2[m, rows, :] = value

        c_piece[rows, :] = score(lambda m: recv1[m, rows, :], a_piece[rows, :], write)
        return carry

    for part in range(2):
        peers(lambda other: exchange(0, part, send1, recv1, other, other).wait_recv())
        first, count = PARTS[part]
        lax.fori_loop(first // 8, (first + count) // 8, score_rows, 0)
        if part == 1:
            rows = slice(LAST, PIECE)

            def write_last(m, value):
                send2[m, rows, :] = value

            c_piece[rows, :] = score(lambda m: recv1[m, rows, :], a_piece[rows, :], write_last)
        peers(lambda other: exchange(1, part, send2, recv2, other, ens).start())
    recv2[ens] = send2[ens]
    stencil_matrices(1, stencils_ref, w_hi, w_lo, spaced, by_row)

    mains = [c_piece[8 + 8 * j : 16 + 8 * j, :] for j in range(TILES)]
    parts = [c_piece[0:8, 32 * j : 32 * j + 32] for j in range(4)]
    for c in range(8):
        row = LAST + c // 4
        parts.append(c_piece[row : row + 1, 32 * (c % 4) : 32 * (c % 4) + 32])
    main = padded(jnp.concatenate(mains, axis=0), 128, 128).T
    tail = padded(jnp.concatenate(parts, axis=0), 128, 128).T
    crps_ref[0:16] = main[:, 0:per].reshape(16, COLS, per)
    crps_ref[16:20] = tail[0:32, 0:per].reshape(4, COLS, per)

    def tile_tail(d, j):
        return recv2[d, 0:8, 32 * j : 32 * j + 32] if j < 4 else tails[d, :, 0:32]

    def returned(step):
        if step < 2:
            peers(lambda other: exchange(1, step, send2, recv2, other, other).wait_recv())
        if step == 1:
            gather_rest(recv2, tails)
        for j in STEPS[step]:
            mains, parts = [], []
            for d in range(n_ens):
                at = slice(8 * (TILES * d + j), 8 * (TILES * d + j) + 8)
                mains.append(recv2[d, 8 + 8 * j : 16 + 8 * j, :] * damp_main[at, :])
                parts.append(tile_tail(d, j) * damp_tail[at, 0:32])
            main = jnp.concatenate(mains, axis=0).T
            tail = padded(jnp.concatenate(parts, axis=0), 128, 128).T
            cols = slice(128 * j, 128 * j + 128)
            field[0:16, :, cols] = main.reshape(16, COLS, 128)
            field[16:20, :, cols] = tail[0:32].reshape(4, COLS, 128)
        cols = slice(128 * STEPS[step][0], 128 * STEPS[step][-1] + 128)
        fill_packs(field, cols)
        start_halo(3 + step, field, cols)

    def adjoint(step):
        inputs = slice(128 * STEPS[step][0], 128 * STEPS[step][-1] + 128)
        extend(3 + step, field, inputs)
        stencil(inputs)
        for cols in chunks():
            more = mix(cols, inputs).reshape(ROWS, COLS, cols.stop - cols.start)
            grad_ref[:, :, cols] = more if step == 0 else grad_ref[:, :, cols] + more

    for step in range(3):
        returned(step)
    adjoint(0)
    adjoint(1)
    for c in range(channels // 128):
        mains, parts = [], []
        for n in range(16):
            k = 16 * c + n
            d, j = k // TILES, k % TILES
            mains.append(recv2[d, 8 + 8 * j : 16 + 8 * j, :])
            parts.append(tile_tail(d, j))
        main = jnp.concatenate(mains, axis=0).T
        tail = padded(jnp.concatenate(parts, axis=0), 128, 128).T
        cols = slice(128 * c, 128 * c + 128)
        grad_ref[0:16, :, cols] = grad_ref[0:16, :, cols] + main.reshape(16, COLS, 128)
        grad_ref[16:20, :, cols] = grad_ref[16:20, :, cols] + tail[0:32].reshape(4, COLS, 128)
    adjoint(2)
    for step, cols in enumerate(chunks()):
        halo_sent(3 + step, field, cols)
    for phase, src, dst in ((0, send1, recv1), (1, send2, recv2)):
        for part in range(2):
            peers(lambda other: exchange(phase, part, src, dst, other, ens).wait_send())


def keep(grad_ref, crps_ref, grad_out, crps_out):
    grad_out[...] = grad_ref[...]
    crps_out[...] = crps_ref[...]


def local(members, analysis, stencils, mixing):
    channels = members.shape[3]
    n_ens = lax.axis_size("ens")
    per = channels // n_ens
    depth = BASES * channels
    cells = ROWS * COLS
    vmem = pl.BlockSpec(memory_space=pltpu.VMEM)
    pieces = pltpu.VMEM((n_ens, PIECE, 128), f32)
    grad, crps = pl.pallas_call(
        step_kernel,
        out_shape=[
            jax.ShapeDtypeStruct((ROWS, COLS, channels), f32),
            jax.ShapeDtypeStruct((ROWS, COLS, per), f32),
        ],
        in_specs=[pl.BlockSpec(memory_space=pl.ANY)] * 4,
        out_specs=[vmem, vmem],
        scratch_shapes=[
            pltpu.VMEM(members.shape[1:], f32),
            pltpu.VMEM(analysis.shape, f32),
            pltpu.VMEM(stencils.shape, f32),
            pltpu.SemaphoreType.DMA((3,)),
            pltpu.VMEM((WINDOWS, 16 * BASES, 128), bf16),
            pltpu.VMEM((WINDOWS, 16 * BASES, 128), bf16),
            pltpu.VMEM((128, 128), f32),
            pltpu.VMEM((128, 128), f32),
            pltpu.VMEM((BASES, channels, channels), f32),
            pltpu.VMEM((channels, channels), f32),
            pltpu.VMEM((depth, channels), bf16),
            pltpu.VMEM((depth, channels), bf16),
            pltpu.VMEM((16 * EXT, channels), bf16),
            pltpu.VMEM((16 * EXT, channels), bf16),
            pltpu.VMEM((cells, depth), bf16),
            pltpu.VMEM((cells, depth), bf16),
            pltpu.VMEM((ROWS, COLS, channels), f32),
            pltpu.VMEM((cells, channels), f32),
            pltpu.VMEM((channels, 128), f32),
            pltpu.VMEM((channels, 128), f32),
            pltpu.VMEM((3 * ROWS, channels), f32),
            pltpu.VMEM((3 * ROWS, channels), f32),
            pltpu.VMEM((9, channels), f32),
            pltpu.VMEM((9, channels), f32),
            pltpu.VMEM((2, 2, 3 * ROWS, channels), f32),
            pltpu.VMEM((2, 2, MARGIN, COLS, channels), f32),
            pltpu.VMEM((2, 2, 12, channels), f32),
            pltpu.VMEM((2, 2, 9, channels), f32),
            pltpu.VMEM((PIECE, 128), f32),
            pltpu.VMEM((PIECE, 128), f32),
            pltpu.VMEM((n_ens, 8, 128), f32),
            pieces, pieces, pieces, pieces,
            pltpu.SemaphoreType.DMA((3,)),
            pltpu.SemaphoreType.DMA((6, 8)),
            pltpu.SemaphoreType.DMA((6, 8)),
            pltpu.SemaphoreType.DMA((2, 2, n_ens)),
            pltpu.SemaphoreType.DMA((2, 2, n_ens)),
        ],
        compiler_params=pltpu.CompilerParams(
            collective_id=0, has_side_effects=True, vmem_limit_bytes=56 * 1024 * 1024
        ),
        name="ensemble_step",
    )(members[0], analysis, stencils, mixing)
    grad, crps = pl.pallas_call(
        keep,
        out_shape=[jax.ShapeDtypeStruct(grad.shape, f32), jax.ShapeDtypeStruct(crps.shape, f32)],
        in_specs=[vmem] * 2,
        out_specs=[vmem] * 2,
        name="results",
    )(grad, crps)
    return grad[None], crps


def solution(mesh):
    in_specs = (P("ens", "lat", "lon", None), P("lat", "lon", "ens"), P(), P())
    out_specs = (P("ens", "lat", "lon", None), P("lat", "lon", "ens"))
    return jax.shard_map(local, mesh=mesh, in_specs=in_specs, out_specs=out_specs, check_vma=False)
```

```python
import functools

import jax
import jax.numpy as jnp
import numpy as np
from jax import lax
from jax.experimental import pallas as pl
from jax.experimental.pallas import tpu as pltpu
from jax.sharding import PartitionSpec as P

BASES = 7
SPAN = 7
MARGIN = 3
ROWS = 20
COLS = 8
WINDOWS = ROWS // 2
EXT = ROWS + 2 * MARGIN
SMOOTH = 0.01
MESH = pl.DeviceIdType.MESH
f32 = jnp.float32
bf16 = jnp.bfloat16


def split(x):
    hi = x.astype(bf16)
    return hi, (x - hi.astype(f32)).astype(bf16)


def mm(a, b):
    return jnp.dot(a, b, preferred_element_type=f32)


def stencil_matrices(kind, st_ref, hi_ref, lo_ref, spaced, by_row):
    lat_rows = st_ref.shape[3]
    first = lax.axis_index("lat") * ROWS
    lane = lax.broadcasted_iota(jnp.int32, (8, 128), 1)
    wrapped = (lane % 16) >= 11
    spaced[...] = jnp.zeros_like(spaced)

    def one_basis(b, carry):
        for p in range(SPAN):
            if kind == 0:
                spaced[16 * p : 16 * p + SPAN, 0:lat_rows] = st_ref[b, p]
            else:
                for q in range(SPAN):
                    r = 16 * p + q
                    spaced[r : r + 1, 0:lat_rows] = st_ref[b, SPAN - 1 - p, SPAN - 1 - q : SPAN - q, :]
        if kind == 0:
            lines = spaced[...]
        else:
            lines = jnp.concatenate(
                [pltpu.roll(spaced[16 * p : 16 * p + 16, :], (MARGIN - p) % 128, 1) for p in range(8)], axis=0
            )
        by_row[...] = pltpu.roll(lines.T, 128 - MARGIN, 1)
        at = pl.ds(pl.multiple_of(16 * b, 16), 16)
        for u in range(WINDOWS):
            rows = []
            for i01 in range(2):
                line = jnp.broadcast_to(by_row[pl.ds(first + 2 * u + i01, 1), :], (8, 128))
                shifted = pltpu.roll(line, 16 * i01, 1, stride=1, stride_axis=0)
                rows.append(jnp.where(wrapped, pltpu.roll(shifted, 16, 1), shifted))
            hi_ref[u, at, :], lo_ref[u, at, :] = split(jnp.concatenate(rows, axis=0))
        return carry

    lax.fori_loop(0, BASES, one_basis, 0)


TILES = 5
LAST = 8 * (TILES + 1)
PIECE = LAST + 2
PARTS = ((0, 24), (24, PIECE - 24))
STEPS = ((0, 1), (2, 3), (4,))


def spread_rest(tails, pieces):
    for c in range(8):
        row = LAST + c // 4
        pieces[:, row, 32 * (c % 4) : 32 * (c % 4) + 32] = tails[:, c, 0:32]


def gather_rest(pieces, tails):
    for c in range(8):
        row = LAST + c // 4
        tails[:, c, 0:32] = pieces[:, row, 32 * (c % 4) : 32 * (c % 4) + 32]


def padded(x, rows, lanes):
    if x.shape[1] < lanes:
        x = jnp.concatenate([x, jnp.zeros((x.shape[0], lanes - x.shape[1]), f32)], axis=1)
    if x.shape[0] < rows:
        x = jnp.concatenate([x, jnp.zeros((rows - x.shape[0], lanes), f32)], axis=0)
    return x


def step_kernel(
    members_hbm, analysis_hbm, stencils_hbm, mixing_ref,
    grad_ref, crps_ref,
    members_ref, analysis_ref, stencils_ref, in_sem,
    w_hi, w_lo, spaced, by_row, staged, turned, m_hi, m_lo, e_hi, e_lo, s_hi, s_lo,
    field, act, damp_main, damp_tail, pack_r, pack_l, low_r, low_l, side, updown, above, below,
    a_piece, c_piece, tails, send1, recv1, send2, recv2,
    mix_sem, halo_send, halo_recv, a2a_send, a2a_recv,
):
    n_ens = lax.axis_size("ens")
    n_lat = lax.axis_size("lat")
    n_lon = lax.axis_size("lon")
    ens, lat, lon = lax.axis_index("ens"), lax.axis_index("lat"), lax.axis_index("lon")
    right, left = lax.rem(lon + 1, n_lon), lax.rem(lon + n_lon - 1, n_lon)
    has_up, has_down = lat > 0, lat < n_lat - 1
    channels = members_hbm.shape[2]
    cells = ROWS * COLS
    per = 8 * TILES

    def chunks():
        return [slice(c, min(c + 256, channels)) for c in range(0, channels, 256)]

    loads = [
        pltpu.make_async_copy(src, dst, in_sem.at[k])
        for k, (src, dst) in enumerate(
            ((members_hbm, members_ref), (stencils_hbm, stencils_ref), (analysis_hbm, analysis_ref))
        )
    ]
    for load in loads:
        load.start()

    def weights_copy(n, cols):
        rows = pl.ds(cols.start, cols.stop - cols.start)
        return pltpu.make_async_copy(mixing_ref.at[:, rows], staged.at[:, rows], mix_sem.at[n])

    for n, cols in enumerate(chunks()):
        weights_copy(n, cols).start()

    barrier = pltpu.get_barrier_semaphore()

    def greet(k, carry):
        pl.semaphore_signal(barrier, 1, device_id={"ens": lax.rem(ens + k, n_ens)}, device_id_type=MESH)
        return carry

    lax.fori_loop(1, n_ens, greet, 0)
    for side_lon in (left, right):
        pl.semaphore_signal(barrier, 1, device_id={"lon": side_lon}, device_id_type=MESH)
    for there, other in ((has_up, lat - 1), (has_down, lat + 1)):
        @pl.when(there)
        def _():
            pl.semaphore_signal(barrier, 1, device_id={"lat": other}, device_id_type=MESH)
            for side_lon in (left, right):
                pl.semaphore_signal(barrier, 1, device_id={"lat": other, "lon": side_lon}, device_id_type=MESH)

    def fill_packs(src, cols):
        for r in range(ROWS):
            pack_r[3 * r : 3 * r + 3, cols] = src[r, COLS - MARGIN : COLS, cols]
            pack_l[3 * r : 3 * r + 3, cols] = src[r, 0:MARGIN, cols]
            if r < MARGIN:
                low_r[3 * r : 3 * r + 3, cols] = src[r, COLS - MARGIN : COLS, cols]
                low_l[3 * r : 3 * r + 3, cols] = src[r, 0:MARGIN, cols]

    every = slice(0, channels)
    for load in loads:
        load.wait()
    fill_packs(members_ref, every)
    pl.semaphore_wait(barrier, n_ens + 1 + 3 * has_up.astype(jnp.int32) + 3 * has_down.astype(jnp.int32))

    def halo_copies(phase, src, cols):
        back = phase // 3
        lanes = pl.ds(cols.start, cols.stop - cols.start)

        def remote(k, a, b, to):
            return pltpu.make_async_remote_copy(
                a, b, halo_send.at[phase, k], halo_recv.at[phase, k], device_id=to, device_id_type=MESH
            )

        up, down = lat - 1, lat + 1
        high = pl.ds(48, 12)
        return [
            (None, None, remote(0, pack_r.at[:, lanes], side.at[back, 0, :, lanes], {"lon": right})),
            (None, None, remote(1, pack_l.at[:, lanes], side.at[back, 1, :, lanes], {"lon": left})),
            (
                has_down, has_up,
                remote(2, src.at[pl.ds(ROWS - 3, 3), :, lanes], updown.at[back, 0, :, :, lanes], {"lat": down}),
            ),
            (
                has_up, has_down,
                remote(3, src.at[pl.ds(0, 3), :, lanes], updown.at[back, 1, :, :, lanes], {"lat": up}),
            ),
            (
                has_down, has_up,
                remote(4, pack_r.at[high, lanes], above.at[back, 0, :, lanes], {"lat": down, "lon": right}),
            ),
            (
                has_down, has_up,
                remote(5, pack_l.at[high, lanes], above.at[back, 1, :, lanes], {"lat": down, "lon": left}),
            ),
            (
                has_up, has_down,
                remote(6, low_r.at[:, lanes], below.at[back, 0, :, lanes], {"lat": up, "lon": right}),
            ),
            (
                has_up, has_down,
                remote(7, low_l.at[:, lanes], below.at[back, 1, :, lanes], {"lat": up, "lon": left}),
            ),
        ]

    def start_halo(phase, src, cols):
        for sends, _, copy in halo_copies(phase, src, cols):
            if sends is None:
                copy.start()
            else:
                pl.when(sends)(copy.start)

    def put_row(r, inner, from_right, from_left, cols):
        gap = jnp.zeros((2, cols.stop - cols.start), f32)
        hi, lo = split(jnp.concatenate([inner, from_right, gap, from_left], axis=0))
        e_hi[16 * r : 16 * r + 16, cols] = hi
        e_lo[16 * r : 16 * r + 16, cols] = lo

    def extend(phase, src, cols):
        copies = halo_copies(phase, src, cols)
        back = phase // 3
        for k in (0, 1):
            copies[k][2].wait_recv()
        for r in range(ROWS):
            at = slice(3 * r, 3 * r + 3)
            put_row(r + MARGIN, src[r, :, cols], side[back, 1, at, cols], side[back, 0, at, cols], cols)
        for there, which, corner, first, offset in (
            (has_up, 0, above, 0, 3),
            (has_down, 1, below, ROWS + MARGIN, 0),
        ):
            @pl.when(there)
            def _():
                for k in (2 + which, 4 + 2 * which, 5 + 2 * which):
                    copies[k][2].wait_recv()
                for r in range(3):
                    at = slice(offset + 3 * r, offset + 3 * r + 3)
                    put_row(
                        first + r, updown[back, which, r, :, cols],
                        corner[back, 1, at, cols], corner[back, 0, at, cols], cols,
                    )

            @pl.when(jnp.logical_not(there))
            def _():
                for ref in (e_hi, e_lo):
                    ref[16 * first : 16 * first + 48, cols] = jnp.zeros((48, cols.stop - cols.start), bf16)

    def halo_sent(phase, src, cols):
        for sends, _, copy in halo_copies(phase, src, cols):
            if sends is None:
                copy.wait_send()
            else:
                pl.when(sends)(copy.wait_send)

    def stencil(cols):
        width = cols.stop - cols.start

        def one_window(u, carry):
            at = pl.ds(pl.multiple_of(32 * u, 32), 128)
            x_hi, x_lo = e_hi[at, cols], e_lo[at, cols]
            wh = w_hi[u]
            out = mm(jnp.concatenate([wh, wh], axis=1), jnp.concatenate([x_hi, x_lo], axis=0)) + mm(w_lo[u], x_hi)
            hi, lo = split(out)
            to = pl.ds(pl.multiple_of(16 * u, 16), 16)
            for b in range(BASES):
                here = slice(BASES * cols.start + b * width, BASES * cols.start + (b + 1) * width)
                s_hi[to, here] = hi[16 * b : 16 * b + 16]
                s_lo[to, here] = lo[16 * b : 16 * b + 16]
            return carry

        lax.fori_loop(0, WINDOWS, one_window, 0, unroll=True)

    def mix(cols, inputs):
        k = slice(BASES * inputs.start, BASES * inputs.stop)
        weights, more = m_hi[k, cols], m_lo[k, cols]
        width = cols.stop - cols.start
        if width == 128:
            both = mm(s_hi[:, k], jnp.concatenate([weights, more], axis=1))
            return both[:, :128] + both[:, 128:] + mm(s_lo[:, k], weights)
        return mm(s_hi[:, k], weights) + mm(s_lo[:, k], weights) + mm(s_hi[:, k], more)

    def load_weights(n, cols):
        weights_copy(n, cols).wait()
        width = cols.stop - cols.start

        def one_basis(b, carry):
            for k in range(width // 128):
                at = cols.start + 128 * k
                hi, lo = split(staged[b, at : at + 128, :])
                to = pl.ds(pl.multiple_of(BASES * cols.start + b * width + 128 * k, 128), 128)
                m_hi[to, :] = hi
                m_lo[to, :] = lo
            return carry

        lax.fori_loop(0, BASES, one_basis, 0)

    def transpose_weights(b, carry):
        for k in range(channels // 128):
            turned[128 * k : 128 * k + 128, :] = staged[b, :, 128 * k : 128 * k + 128].T
        for first, tiles in ((128 * step[0], step) for step in STEPS):
            width = 128 * len(tiles)
            for n, j in enumerate(tiles):
                for d in range(0, n_ens, 2):
                    low, high = 8 * (TILES * d + j), 8 * (TILES * (d + 1) + j)
                    hi, lo = split(jnp.concatenate([turned[low : low + 8, :], turned[high : high + 8, :]], axis=0))
                    to = pl.ds(pl.multiple_of(BASES * first + b * width + 128 * n + 8 * d, 16), 16)
                    m_hi[to, :] = hi
                    m_lo[to, :] = lo
        return carry

    for n, cols in enumerate(chunks()):
        start_halo(n, members_ref, cols)
    stencil_matrices(0, stencils_ref, w_hi, w_lo, spaced, by_row)

    for n, inputs in enumerate(chunks()):
        load_weights(n, inputs)
        extend(n, members_ref, inputs)
        stencil(inputs)

    def exchange(phase, part, src, dst, other, slot):
        first, count = PARTS[part]
        rows = pl.ds(first, count)
        return pltpu.make_async_remote_copy(
            src.at[other, rows], dst.at[slot, rows], a2a_send.at[phase, part, other], a2a_recv.at[phase, part, slot],
            device_id={"ens": other}, device_id_type=MESH,
        )

    def peers(action):
        def one(k, carry):
            action(lax.rem(ens + k, n_ens))
            return carry

        lax.fori_loop(1, n_ens, one, 0, unroll=True)

    for cols in chunks():
        width = cols.stop - cols.start
        activation = jnp.tanh(mix(cols, every))
        act[:, cols] = activation
        forecast = members_ref[:, :, cols].reshape(cells, width) + activation
        for c in range(width // 128):
            part = forecast[:, 128 * c : 128 * c + 128]
            main, tail = part[:128].T, padded(part[128:], 128, 128).T
            for n in range(16):
                k = (cols.start // 128 + c) * 16 + n
                d, j = k // TILES, k % TILES
                send1[d, 8 + 8 * j : 16 + 8 * j, :] = main[8 * n : 8 * n + 8]
                if j < 4:
                    send1[d, 0:8, 32 * j : 32 * j + 32] = tail[8 * n : 8 * n + 8, 0:32]
                else:
                    tails[d, :, 0:32] = tail[8 * n : 8 * n + 8, 0:32]
    peers(lambda other: exchange(0, 0, send1, recv1, other, ens).start())
    spread_rest(tails, send1)
    peers(lambda other: exchange(0, 1, send1, recv1, other, ens).start())
    recv1[ens] = send1[ens]

    for n, cols in enumerate(chunks()):
        halo_sent(n, members_ref, cols)

    truth = padded(analysis_ref[...].reshape(cells, per), cells, 128)
    main, tail = truth[:128].T, padded(truth[128:], 128, 128).T
    for j in range(TILES):
        a_piece[8 + 8 * j : 16 + 8 * j, :] = main[8 * j : 8 * j + 8]
        if j < 4:
            a_piece[0:8, 32 * j : 32 * j + 32] = tail[8 * j : 8 * j + 8, 0:32]
        else:
            for c in range(8):
                row = LAST + c // 4
                a_piece[row : row + 1, 32 * (c % 4) : 32 * (c % 4) + 32] = tail[8 * j + c : 8 * j + c + 1, 0:32]

    lax.fori_loop(0, BASES, transpose_weights, 0)
    members_total = n_ens
    diagonal = members_total * float(np.sqrt(np.float32(SMOOTH)))
    pairs_scale = 2.0 * members_total * (members_total - 1)

    def score(read, truth, write):
        x = [read(m) - truth for m in range(n_ens)]
        slope = [None] * n_ens
        own, pair_abs = None, None
        for m in range(n_ens):
            for n in range(m + 1, n_ens):
                d = x[m] - x[n]
                s2 = d * d + SMOOTH
                r = lax.rsqrt(s2)
                sl = d * r
                ab = s2 * r
                pair_abs = ab if pair_abs is None else pair_abs + ab
                slope[m] = sl if slope[m] is None else slope[m] + sl
                slope[n] = -sl if slope[n] is None else slope[n] - sl
            s2 = x[m] * x[m] + SMOOTH
            r = lax.rsqrt(s2)
            own = s2 * r if own is None else own + s2 * r
            write(m, x[m] * r - slope[m] * (1.0 / (members_total - 1.0)))
        return own * (1.0 / members_total) - (2.0 * pair_abs + diagonal) * (1.0 / pairs_scale)

    def score_rows(t, carry):
        rows = pl.ds(pl.multiple_of(8 * t, 8), 8)

        def write(m, value):
            send2[m, rows, :] = value

        c_piece[rows, :] = score(lambda m: recv1[m, rows, :], a_piece[rows, :], write)
        return carry

    for part in range(2):
        peers(lambda other: exchange(0, part, send1, recv1, other, other).wait_recv())
        first, count = PARTS[part]
        lax.fori_loop(first // 8, (first + count) // 8, score_rows, 0)
        if part == 1:
            rows = slice(LAST, PIECE)

            def write_last(m, value):
                send2[m, rows, :] = value

            c_piece[rows, :] = score(lambda m: recv1[m, rows, :], a_piece[rows, :], write_last)
        peers(lambda other: exchange(1, part, send2, recv2, other, ens).start())
    recv2[ens] = send2[ens]
    for c in range(channels // 128):
        damp = act[:, 128 * c : 128 * c + 128]
        damp = 1.0 - damp * damp
        damp_main[128 * c : 128 * c + 128, :] = damp[:128].T
        damp_tail[128 * c : 128 * c + 128, :] = padded(damp[128:], 128, 128).T
    stencil_matrices(1, stencils_ref, w_hi, w_lo, spaced, by_row)

    mains = [c_piece[8 + 8 * j : 16 + 8 * j, :] for j in range(TILES)]
    parts = [c_piece[0:8, 32 * j : 32 * j + 32] for j in range(4)]
    for c in range(8):
        row = LAST + c // 4
        parts.append(c_piece[row : row + 1, 32 * (c % 4) : 32 * (c % 4) + 32])
    main = padded(jnp.concatenate(mains, axis=0), 128, 128).T
    tail = padded(jnp.concatenate(parts, axis=0), 128, 128).T
    crps_ref[0:16] = main[:, 0:per].reshape(16, COLS, per)
    crps_ref[16:20] = tail[0:32, 0:per].reshape(4, COLS, per)

    def tile_tail(d, j):
        return recv2[d, 0:8, 32 * j : 32 * j + 32] if j < 4 else tails[d, :, 0:32]

    def returned(step):
        if step < 2:
            peers(lambda other: exchange(1, step, send2, recv2, other, other).wait_recv())
        if step == 1:
            gather_rest(recv2, tails)
        for j in STEPS[step]:
            mains, parts = [], []
            for d in range(n_ens):
                at = slice(8 * (TILES * d + j), 8 * (TILES * d + j) + 8)
                mains.append(recv2[d, 8 + 8 * j : 16 + 8 * j, :] * damp_main[at, :])
                parts.append(tile_tail(d, j) * damp_tail[at, 0:32])
            main = jnp.concatenate(mains, axis=0).T
            tail = padded(jnp.concatenate(parts, axis=0), 128, 128).T
            cols = slice(128 * j, 128 * j + 128)
            field[0:16, :, cols] = main.reshape(16, COLS, 128)
            field[16:20, :, cols] = tail[0:32].reshape(4, COLS, 128)
        cols = slice(128 * STEPS[step][0], 128 * STEPS[step][-1] + 128)
        fill_packs(field, cols)
        start_halo(3 + step, field, cols)

    def adjoint(step):
        inputs = slice(128 * STEPS[step][0], 128 * STEPS[step][-1] + 128)
        extend(3 + step, field, inputs)
        stencil(inputs)
        for cols in chunks():
            more = mix(cols, inputs).reshape(ROWS, COLS, cols.stop - cols.start)
            grad_ref[:, :, cols] = more if step == 0 else grad_ref[:, :, cols] + more

    for step in range(3):
        returned(step)
    adjoint(0)
    adjoint(1)
    for c in range(channels // 128):
        mains, parts = [], []
        for n in range(16):
            k = 16 * c + n
            d, j = k // TILES, k % TILES
            mains.append(recv2[d, 8 + 8 * j : 16 + 8 * j, :])
            parts.append(tile_tail(d, j))
        main = jnp.concatenate(mains, axis=0).T
        tail = padded(jnp.concatenate(parts, axis=0), 128, 128).T
        cols = slice(128 * c, 128 * c + 128)
        grad_ref[0:16, :, cols] = grad_ref[0:16, :, cols] + main.reshape(16, COLS, 128)
        grad_ref[16:20, :, cols] = grad_ref[16:20, :, cols] + tail[0:32].reshape(4, COLS, 128)
    adjoint(2)
    for step, cols in enumerate(chunks()):
        halo_sent(3 + step, field, cols)
    for phase, src, dst in ((0, send1, recv1), (1, send2, recv2)):
        for part in range(2):
            peers(lambda other: exchange(phase, part, src, dst, other, ens).wait_send())


def keep(grad_ref, crps_ref, grad_out, crps_out):
    grad_out[...] = grad_ref[...]
    crps_out[...] = crps_ref[...]


def local(members, analysis, stencils, mixing):
    channels = members.shape[3]
    n_ens = lax.axis_size("ens")
    per = channels // n_ens
    depth = BASES * channels
    cells = ROWS * COLS
    vmem = pl.BlockSpec(memory_space=pltpu.VMEM)
    pieces = pltpu.VMEM((n_ens, PIECE, 128), f32)
    grad, crps = pl.pallas_call(
        step_kernel,
        out_shape=[
            jax.ShapeDtypeStruct((ROWS, COLS, channels), f32),
            jax.ShapeDtypeStruct((ROWS, COLS, per), f32),
        ],
        in_specs=[pl.BlockSpec(memory_space=pl.ANY)] * 4,
        out_specs=[vmem, vmem],
        scratch_shapes=[
            pltpu.VMEM(members.shape[1:], f32),
            pltpu.VMEM(analysis.shape, f32),
            pltpu.VMEM(stencils.shape, f32),
            pltpu.SemaphoreType.DMA((3,)),
            pltpu.VMEM((WINDOWS, 16 * BASES, 128), bf16),
            pltpu.VMEM((WINDOWS, 16 * BASES, 128), bf16),
            pltpu.VMEM((128, 128), f32),
            pltpu.VMEM((128, 128), f32),
            pltpu.VMEM((BASES, channels, channels), f32),
            pltpu.VMEM((channels, channels), f32),
            pltpu.VMEM((depth, channels), bf16),
            pltpu.VMEM((depth, channels), bf16),
            pltpu.VMEM((16 * EXT, channels), bf16),
            pltpu.VMEM((16 * EXT, channels), bf16),
            pltpu.VMEM((cells, depth), bf16),
            pltpu.VMEM((cells, depth), bf16),
            pltpu.VMEM((ROWS, COLS, channels), f32),
            pltpu.VMEM((cells, channels), f32),
            pltpu.VMEM((channels, 128), f32),
            pltpu.VMEM((channels, 128), f32),
            pltpu.VMEM((3 * ROWS, channels), f32),
            pltpu.VMEM((3 * ROWS, channels), f32),
            pltpu.VMEM((9, channels), f32),
            pltpu.VMEM((9, channels), f32),
            pltpu.VMEM((2, 2, 3 * ROWS, channels), f32),
            pltpu.VMEM((2, 2, MARGIN, COLS, channels), f32),
            pltpu.VMEM((2, 2, 12, channels), f32),
            pltpu.VMEM((2, 2, 9, channels), f32),
            pltpu.VMEM((PIECE, 128), f32),
            pltpu.VMEM((PIECE, 128), f32),
            pltpu.VMEM((n_ens, 8, 128), f32),
            pieces, pieces, pieces, pieces,
            pltpu.SemaphoreType.DMA((3,)),
            pltpu.SemaphoreType.DMA((6, 8)),
            pltpu.SemaphoreType.DMA((6, 8)),
            pltpu.SemaphoreType.DMA((2, 2, n_ens)),
            pltpu.SemaphoreType.DMA((2, 2, n_ens)),
        ],
        compiler_params=pltpu.CompilerParams(
            collective_id=0, has_side_effects=True, vmem_limit_bytes=56 * 1024 * 1024
        ),
        name="ensemble_step",
    )(members[0], analysis, stencils, mixing)
    grad, crps = pl.pallas_call(
        keep,
        out_shape=[jax.ShapeDtypeStruct(grad.shape, f32), jax.ShapeDtypeStruct(crps.shape, f32)],
        in_specs=[vmem] * 2,
        out_specs=[vmem] * 2,
        name="results",
    )(grad, crps)
    return grad[None], crps


def solution(mesh):
    in_specs = (P("ens", "lat", "lon", None), P("lat", "lon", "ens"), P(), P())
    out_specs = (P("ens", "lat", "lon", None), P("lat", "lon", "ens"))
    return jax.shard_map(local, mesh=mesh, in_specs=in_specs, out_specs=out_specs, check_vma=False)
```
